128 devices in a mesh: grp: 8 (over z, core), blk: 16 (over x, y).
Axes of the slice: x: 4, y: 4, z: 4, core: 2. Of those that a mesh axis runs over, the one named last changes fastest.
Arguments:
- chol_done: float32 [622592, 512], P(('grp', 'blk')), as said below
- new_cols: float32 [622592, 384], P(('grp', 'blk')), as said below
- diag_entries: float32 [622592], P(('grp', 'blk')), as said below
- pivots: int32 [2, 192], replicated, may hold values from 0 to 622591, as said below
- live_blocks: int32 [128], replicated, may hold values from 1 to 19, as said below
Outputs:
- new_vectors: float32 [622592, 384], P(('grp', 'blk'))
- left_ratio: float32 [1], replicated
The draws below stay inside these ranges and needn't reach their ends.
Inputs may be any that keep to these rules, and one draw needn't show every extreme that they name: The pivots of both panels are 384 distinct pair rows, all screened in; each device's rows hold at most 3 pivots of one panel, and some device holds exactly 3 in each panel. `live_blocks`: some device has all its blocks screened in; the screened-in blocks of a device come first. `chol_done`: rows of screened-out blocks are zero. `new_cols`: rows of screened-out blocks are zero; each panel's block at its pivot rows, after all earlier vectors are subtracted, is symmetric positive definite. `diag_entries`: entries of screened-out rows are zero.
All inputs are finite; a program needn't handle non-finite values.
Results may differ from the reference program's by a relative error of at most 0.00011.
Values sent between devices are 32-bit elements; how exact they have to be, the bound alone decides.
A program may use at most 128 MiB of HBM per device.

```python
import jax
import jax.numpy as jnp
from jax import lax

K = 512
P_SIZE = 192
BLOCK_ROWS = 256
ROWS_DEV = 4864
DEVICES = 128


def layout_parts(key):
    total_blocks = ROWS_DEV // BLOCK_ROWS
    pmax = (2 * P_SIZE + DEVICES - 1) // DEVICES
    base = jax.random.fold_in(key, 7001)
    shifts = jax.random.randint(jax.random.fold_in(base, 1), (DEVICES,), 0, 3)
    counts = jnp.maximum(jnp.right_shift(jnp.full((DEVICES,), total_blocks, jnp.int32), shifts), 1)
    fullest = jax.random.randint(jax.random.fold_in(base, 2), (), 0, DEVICES)
    counts = counts.at[fullest].set(total_blocks).astype(jnp.int32)
    slots = DEVICES * pmax
    chosen = []
    for panel_id in range(2):
        pkey = jax.random.fold_in(base, 10 + panel_id)
        score = jax.random.permutation(jax.random.fold_in(pkey, 1), slots).astype(jnp.int32)
        busiest = jax.random.randint(jax.random.fold_in(pkey, 2), (), 0, DEVICES)
        slot_ids = jnp.arange(slots, dtype=jnp.int32)
        score = jnp.where(slot_ids // pmax == busiest, -1 - slot_ids % pmax, score)
        picked = jnp.argsort(score, stable=True)[:P_SIZE].astype(jnp.int32)
        device = picked // pmax
        within = picked % pmax
        span = counts[device] * BLOCK_ROWS // (2 * pmax)
        offset = jax.random.randint(jax.random.fold_in(pkey, 3), (P_SIZE,), 0, span)
        row = (panel_id * pmax + within) * span + offset
        chosen.append(device * ROWS_DEV + row)
    return (counts, jnp.stack(chosen).astype(jnp.int32))


def float_parts(key):
    counts, pivot_rows = layout_parts(key)
    total = ROWS_DEV * DEVICES
    rows_index = jnp.arange(total)
    owner = rows_index // ROWS_DEV
    mask = (rows_index - owner * ROWS_DEV < counts[owner] * BLOCK_ROWS).astype(jnp.float32)
    base = jax.random.fold_in(key, 9001)
    low = jnp.clip(jax.random.normal(jax.random.fold_in(base, 1), (total, K), jnp.float32), -5.0, 5.0) * 0.5
    low = low * mask[:, None]
    rise = 1.0 + 2.0 * owner.astype(jnp.float32) / max(DEVICES - 1, 1)
    rough = jax.random.uniform(jax.random.fold_in(base, 2), (total,), jnp.float32, 0.7, 1.3)
    extra = jax.random.normal(jax.random.fold_in(base, 3), (total, 2 * P_SIZE), jnp.float32) * (10.0 / (2 * P_SIZE) ** 0.5)
    extra = extra * (rise * rough * mask)[:, None]
    columns = []
    for panel_id in range(2):
        piv = pivot_rows[panel_id]
        part = jnp.dot(low, low[piv].T, precision=lax.Precision.HIGHEST)
        part = part + jnp.dot(extra, extra[piv].T, precision=lax.Precision.HIGHEST)
        part = part.at[piv, jnp.arange(P_SIZE)].add(100.0)
        columns.append(part)
    marked = jnp.zeros((total,), jnp.float32).at[pivot_rows.reshape(-1)].set(100.0)
    diagonal = jnp.sum(low * low, axis=1) + jnp.sum(extra * extra, axis=1) + marked
    return (low, jnp.concatenate(columns, axis=1), diagonal)


def draw_live_blocks(key, part):
    return layout_parts(key)[0]


def draw_pivots(key, part):
    return layout_parts(key)[1]


def draw_chol_done(key, part):
    return float_parts(key)[0]


def draw_new_cols(key, part):
    return float_parts(key)[1]


def draw_diag_entries(key, part):
    return float_parts(key)[2]


def setup_inputs(seed: int = 0) -> dict:
    keys = jax.random.split(jax.random.key(seed), 6)
    chol_done = draw_chol_done(jax.random.fold_in(keys[5], 71), 0)
    new_cols = draw_new_cols(jax.random.fold_in(keys[5], 71), 0)
    diag_entries = draw_diag_entries(jax.random.fold_in(keys[5], 71), 0)
    pivots = draw_pivots(jax.random.fold_in(keys[5], 71), 0)
    live_blocks = draw_live_blocks(jax.random.fold_in(keys[5], 71), 0)
    return dict(chol_done=chol_done, new_cols=new_cols, diag_entries=diag_entries, pivots=pivots, live_blocks=live_blocks)


def live_mask(live_blocks, total):
    rows_index = jnp.arange(total)
    owner = rows_index // ROWS_DEV
    return (rows_index - owner * ROWS_DEV < live_blocks[owner] * BLOCK_ROWS).astype(jnp.float32)

def panel(cols, pivot_set, factors, mask):
    resid = cols
    for factor in factors:
        resid = resid - jnp.dot(factor, factor[pivot_set].T, precision=lax.Precision.HIGHEST)
    resid = resid * mask[:, None]
    lower = jnp.linalg.cholesky(resid[pivot_set])
    inverse = lax.linalg.triangular_solve(lower, jnp.eye(P_SIZE, dtype=jnp.float32), left_side=True, lower=True)
    return jnp.dot(resid, inverse.T, precision=lax.Precision.HIGHEST)

def reference(chol_done, new_cols, diag_entries, pivots, live_blocks):
    mask = live_mask(live_blocks, chol_done.shape[0])
    first = panel(new_cols[:, :P_SIZE], pivots[0], (chol_done,), mask)
    second = panel(new_cols[:, P_SIZE:], pivots[1], (chol_done, first), mask)
    left = diag_entries - jnp.sum(chol_done * chol_done, axis=1)
    left = left - jnp.sum(first * first, axis=1)
    left = (left - jnp.sum(second * second, axis=1)) * mask
    ratio = jnp.max(left) / jnp.max(diag_entries * mask)
    return (jnp.concatenate([first, second], axis=1), ratio.reshape(1))
```

```python
import jax
import jax.numpy as jnp
from jax import lax
from jax.experimental import pallas as pl
from jax.experimental.pallas import tpu as pltpu
from jax.sharding import PartitionSpec as P

MESH = pl.DeviceIdType.MESH
HIGHEST = lax.Precision.HIGHEST
F32 = jnp.float32
BF16 = jnp.bfloat16
ROWS = 4864
K = 512
ORDER = 192
COLS = 384
BLOCK_ROWS = 256
SLOTS = 3
SLOT_ROWS = 40
STEP = 16
ROUNDS = ORDER // STEP
TILE = 384
LAST = ROWS - ROUNDS * TILE
CHUNKS = [(i * TILE, TILE) for i in range(ROUNDS)] + [(ROUNDS * TILE, LAST)]
VMEM_LIMIT = 60 * 1024 * 1024
COLOURS = ((0, 16, "yxz"), (16, 16, "xzy"), (32, 8, "zyx"))


def slot_base(panel, slot):
    return slot * 6 if panel == 0 else 18 + slot * 7


def pick_kernel(piv_ref, chol_hbm, cols_hbm, out_ref, cbuf, nbuf, sem):
    me = lax.axis_index("grp") * 16 + lax.axis_index("blk")
    base = me * ROWS
    local = piv_ref[...] - base
    mine = (local >= 0) & (local < ROWS)
    spot = lax.broadcasted_iota(jnp.int32, (2, ORDER), 1)
    key = jnp.where(mine, (spot * 8192 + local).astype(F32), 4.0e6)
    found = []
    for slot in range(SLOTS):
        least = jnp.min(key, axis=1, keepdims=True)
        found.append(least)
        key = jnp.where(key <= least, 4.0e6, key)
    copies = []
    where_row = []
    for panel in range(2):
        for slot in range(SLOTS):
            value = found[slot][panel, 0].astype(jnp.int32)
            row = jnp.where(value < 4000000, value & 8191, 0)
            row = jnp.minimum(row, ROWS - 1)
            group = pl.multiple_of((row // 8) * 8, 8)
            n = panel * SLOTS + slot
            one = pltpu.make_async_copy(chol_hbm.at[pl.ds(group, 8)], cbuf.at[n], sem.at[0, n])
            two = pltpu.make_async_copy(cols_hbm.at[pl.ds(group, 8)], nbuf.at[n], sem.at[1, n])
            one.start()
            two.start()
            copies.append((one, two))
            where_row.append(row - group)
    for panel in range(2):
        for slot in range(SLOTS):
            n = panel * SLOTS + slot
            for copy in copies[n]:
                copy.wait()
            at = slot_base(panel, slot)
            sub = lax.broadcasted_iota(jnp.int32, (8, 128), 0) == where_row[n]
            for c in range(6 if panel == 0 else 7):
                tile = cbuf[n, :, c * 128 : c * 128 + 128] if c < 4 else nbuf[n, :, (c - 4) * 128 : (c - 3) * 128]
                out_ref[at + c : at + c + 1, :] = jnp.sum(jnp.where(sub, tile, 0.0), axis=0, keepdims=True)
    out_ref[39:40, :] = jnp.zeros((1, 128), F32)


def pick(pivots, chol_done, new_cols):
    return pl.pallas_call(
        pick_kernel,
        out_shape=jax.ShapeDtypeStruct((SLOT_ROWS, 128), F32),
        in_specs=[
            pl.BlockSpec(memory_space=pltpu.VMEM),
            pl.BlockSpec(memory_space=pl.ANY),
            pl.BlockSpec(memory_space=pl.ANY),
        ],
        out_specs=pl.BlockSpec(memory_space=pltpu.VMEM),
        scratch_shapes=[
            pltpu.VMEM((6, 8, K), F32),
            pltpu.VMEM((6, 8, COLS), F32),
            pltpu.SemaphoreType.DMA((2, 6)),
        ],
    )(pivots, chol_done, new_cols)


def gather_kernel(in_ref, g_ref, own_sem, send_sem, recv_sem, pass_send, pass_recv):
    grp, blk = lax.axis_index("grp"), lax.axis_index("blk")
    at = {"z": lax.div(grp, 2), "x": lax.div(blk, 4), "y": lax.rem(blk, 4)}
    core = lax.rem(grp, 2)

    def device(z, c, x, y):
        return (z * 2 + c, x * 4 + y)

    def beside(axis, k):
        there = dict(at)
        there[axis] = lax.rem(at[axis] + k, 4)
        return device(there["z"], core, there["x"], there["y"])

    partner = device(at["z"], 1 - core, at["x"], at["y"])
    barrier = pltpu.get_barrier_semaphore()
    for axis in "xyz":
        for k in (1, 2, 3):
            pl.semaphore_signal(barrier, inc=1, device_id=beside(axis, k), device_id_type=MESH)
    pl.semaphore_signal(barrier, inc=1, device_id=partner, device_id_type=MESH)
    own = pltpu.make_async_copy(in_ref, g_ref.at[at["z"], core, at["x"], at["y"]], own_sem)
    own.start()
    pl.semaphore_wait(barrier, 10)

    def region(colour, have, fixed):
        first, count, _ = COLOURS[colour]
        pick_at = [slice(None) if a in have else fixed[a] for a in "zxy"]
        return g_ref.at[pick_at[0], core, pick_at[1], pick_at[2], pl.ds(first, count), :]

    flights = {}

    def launch(colour, phase):
        first, count, order = COLOURS[colour]
        have = order[:phase]
        here = region(colour, have, at)
        for k in (2, 1, 3):
            source = in_ref.at[pl.ds(first, count), :] if phase == 0 else here
            copy = pltpu.make_async_remote_copy(
                src_ref=source,
                dst_ref=here,
                send_sem=send_sem.at[colour, phase, k - 1],
                recv_sem=recv_sem.at[colour, phase, k - 1],
                device_id=beside(order[phase], k),
                device_id_type=MESH,
            )
            copy.start()
            flights[colour, phase, k] = copy

    passes = []

    def hand_over(colour, piece, ref):
        copy = pltpu.make_async_remote_copy(
            src_ref=ref,
            dst_ref=ref,
            send_sem=pass_send.at[colour, piece],
            recv_sem=pass_recv.at[colour, piece],
            device_id=partner,
            device_id_type=MESH,
        )
        copy.start()
        passes.append(copy)

    colours = range(len(COLOURS))
    for colour in colours:
        launch(colour, 0)
    own.wait()
    for phase in (1, 2):
        for colour in colours:
            for k in (1, 3, 2):
                flights[colour, phase - 1, k].wait_recv()
            launch(colour, phase)
            if phase == 2:
                hand_over(colour, 0, region(colour, COLOURS[colour][2][:2], at))
    for k in (1, 3, 2):
        for colour in colours:
            flights[colour, 2, k].wait_recv()
            last = COLOURS[colour][2][2]
            there = dict(at)
            there[last] = lax.rem(at[last] + (4 - k), 4)
            hand_over(colour, k, region(colour, COLOURS[colour][2][:2], there))
    for copy in passes:
        copy.wait_recv()
    for copy in passes:
        copy.wait_send()
    for copy in flights.values():
        copy.wait_send()


def gather(slots):
    return pl.pallas_call(
        gather_kernel,
        out_shape=jax.ShapeDtypeStruct((4, 2, 4, 4, SLOT_ROWS, 128), F32),
        in_specs=[pl.BlockSpec(memory_space=pltpu.VMEM)],
        out_specs=pl.BlockSpec(memory_space=pltpu.VMEM),
        scratch_shapes=[
            pltpu.SemaphoreType.DMA,
            pltpu.SemaphoreType.DMA((3, 3, 3)),
            pltpu.SemaphoreType.DMA((3, 3, 3)),
            pltpu.SemaphoreType.DMA((3, 4)),
            pltpu.SemaphoreType.DMA((3, 4)),
        ],
        compiler_params=pltpu.CompilerParams(collective_id=0, has_side_effects=True),
    )(slots)


def split2(a):
    high = a.astype(BF16)
    return high, (a - high.astype(F32)).astype(BF16)


def split3(a):
    high = a.astype(BF16)
    rest = a - high.astype(F32)
    mid = rest.astype(BF16)
    return high, mid, (rest - mid.astype(F32)).astype(BF16)


def mul(a, b):
    return jnp.dot(a, b, preferred_element_type=F32)


def mul3(a, b_high, b_low):
    high, low = split2(a)
    return mul(high, b_high) + (mul(high, b_low) + mul(low, b_high))


def exact(a, b):
    return jnp.dot(a, b, precision=HIGHEST, preferred_element_type=F32)


def over_lanes(x, lane):
    return jnp.take_along_axis(x, jnp.full((8, 128), lane, jnp.int32), axis=1)


def over_rows(x, row):
    return jnp.broadcast_to(x[row : row + 1, :], (8, 128))


def factor_round(a_ref, r, off):
    rs = pl.multiple_of(r * STEP, STEP)
    c0 = off + r * STEP
    t = c0 // 128
    l0 = c0 - t * 128
    tl = pl.multiple_of(t * 128, 128)
    lane = lax.broadcasted_iota(jnp.int32, (8, 128), 1)
    sub = lax.broadcasted_iota(jnp.int32, (8, 128), 0)
    raw = [a_ref[pl.ds(rs + 8 * q, 8), pl.ds(tl, 128)] for q in range(2)]
    col = {}
    for j in range(STEP):
        for q in range(j // 8, 2):
            col[j, q] = over_lanes(raw[q], l0 + j)
    row = {}
    for q in range(2):
        for h in range(2):
            x = a_ref[pl.ds(rs + 8 * q, 8), h * 128 : (h + 1) * 128]
            rel = lane + (h * 128) - c0
            unit = jnp.where(rel == sub + 8 * q, 1.0, 0.0)
            row[q, h] = jnp.where((rel >= 0) & (rel < STEP), unit, x)
    for j in range(STEP):
        jq, js = j // 8, j % 8
        scale = lax.rsqrt(over_rows(col[j, jq], js))
        low = {q: col[j, q] * scale for q in range(jq, 2)}
        for m in range(j + 1, STEP):
            times = over_rows(low[m // 8], m % 8)
            for q in range(m // 8, 2):
                col[m, q] = col[m, q] - low[q] * times
        low[jq] = jnp.where(sub > js, low[jq], 0.0)
        for h in range(2):
            lead = over_rows(row[jq, h], js) * scale
            for q in range(jq, 2):
                row[q, h] = row[q, h] - low[q] * lead
            row[jq, h] = jnp.where(sub == js, lead, row[jq, h])
    for q in range(2):
        for h in range(2):
            a_ref[pl.ds(rs + 8 * q, 8), h * 128 : (h + 1) * 128] = row[q, h]
    u = jnp.concatenate([jnp.concatenate([row[q, h] for h in range(2)], axis=1) for q in range(2)], axis=0)
    lanes = lax.broadcasted_iota(jnp.int32, (STEP, 256), 1)
    high, mid, low3 = split3(u)
    zero = jnp.zeros_like(u)
    ahead = lanes >= c0 + STEP
    h_l, m_l, l_l = split3(jnp.where(ahead, u, zero))
    left = jnp.concatenate([h_l, h_l, m_l, m_l, h_l, l_l], axis=0)
    right = jnp.concatenate([high, mid, high, mid, low3, high], axis=0)
    z = lax.dot_general(left, right, (((0,), (0,)), ((), ())), preferred_element_type=F32)
    rows_i = lax.broadcasted_iota(jnp.int32, (ORDER, 256), 0)
    cols_i = lax.broadcasted_iota(jnp.int32, (ORDER, 256), 1)
    old = (rows_i >= rs + STEP) & (cols_i >= c0) & (cols_i < c0 + STEP)
    a_ref[...] = jnp.where(old, 0.0, a_ref[...]) - z[off : off + ORDER, :]


def lower_only(a, off):
    row = lax.broadcasted_iota(jnp.int32, (ORDER, 256), 0)
    col = lax.broadcasted_iota(jnp.int32, (ORDER, 256), 1) - off
    return jnp.where((col >= 0) & (col <= row), a, 0.0)


def panel_kernel(g_ref, piv_ref, live_ref, diag_ref, chol_hbm, cols_hbm, out_hbm, top_ref,
                 chol, rbuf, squares, hmat, htr, ht_high, ht_low, head, a_ref,
                 v_high, v_low, f_high, f_low, sums, in_sem, out_sem):
    me = lax.axis_index("grp") * 16 + lax.axis_index("blk")
    alive = live_ref[me] * BLOCK_ROWS

    def fetch(start, count, n):
        rows = pl.ds(start, count)
        return (
            pltpu.make_async_copy(chol_hbm.at[rows], chol.at[rows], in_sem.at[0, n]),
            pltpu.make_async_copy(cols_hbm.at[rows], rbuf.at[rows], in_sem.at[1, n]),
        )

    for n, (start, count) in enumerate(CHUNKS):
        for copy in fetch(start, count, n):
            copy.start()

    q_i = lax.broadcasted_iota(jnp.int32, (ORDER, ORDER), 1)
    p_i = lax.broadcasted_iota(jnp.int32, (ORDER, ORDER), 0)
    for panel in range(2):
        owner_row = (piv_ref[panel : panel + 1, :] // ROWS).astype(F32)
        owner_all = jnp.broadcast_to(owner_row, (ORDER, ORDER))
        owner = jnp.sum(jnp.where(q_i == p_i, owner_all, 0.0), axis=1, keepdims=True)
        before = (owner_all == owner) & (q_i < p_i)
        rank = jnp.sum(jnp.where(before, 1.0, 0.0), axis=1, keepdims=True)
        dev = lax.broadcasted_iota(jnp.int32, (ORDER, 128), 1).astype(F32)
        hot = jnp.concatenate(
            [jnp.where((dev == owner) & (rank == float(s)), 1.0, 0.0) for s in range(SLOTS)], axis=1
        ).astype(BF16)
        for c in range(6 if panel == 0 else 7):
            pieces = [g_ref[pl.ds(slot_base(panel, s) + c, 128, stride=SLOT_ROWS), :] for s in range(SLOTS)]
            high, mid, low = split3(jnp.concatenate(pieces, axis=0))
            rows = mul(hot, high) + (mul(hot, mid) + mul(hot, low))
            if c < 4:
                hmat[panel * ORDER : (panel + 1) * ORDER, c * 128 : (c + 1) * 128] = rows
            else:
                head[panel, :, (c - 4) * 128 : (c - 3) * 128] = rows
    htr[...] = hmat[...].T
    high, low = split2(htr[...])
    ht_high[...] = high
    ht_low[...] = low

    lanes = lax.broadcasted_iota(jnp.int32, (ORDER, 256), 1)
    one = head[0, :, 0:256] - exact(hmat[0:ORDER, :], htr[:, 0:256])
    a_ref[...] = jnp.where(lanes < ORDER, one, 0.0)

    def residual(start, count):
        rows = pl.ds(start, count)
        tile = chol[rows, :]
        left = rbuf[rows, :] - mul3(tile, ht_high[...], ht_low[...])
        spot = lax.broadcasted_iota(jnp.int32, (count, COLS), 0) + start
        rbuf[rows, :] = jnp.where(spot < alive, left, 0.0)
        square = tile * tile
        squares[rows, :] = (square[:, 0:128] + square[:, 128:256]) + (square[:, 256:384] + square[:, 384:512])

    def round_one(r, _):
        start = pl.multiple_of(r * TILE, TILE)
        for copy in fetch(start, TILE, r):
            copy.wait()
        factor_round(a_ref, r, 0)
        residual(start, TILE)
        return 0

    lax.fori_loop(0, ROUNDS, round_one, 0)
    for copy in fetch(ROUNDS * TILE, LAST, ROUNDS):
        copy.wait()
    residual(ROUNDS * TILE, LAST)

    pad = jnp.zeros((64, 256), F32)
    v_one = jnp.concatenate([lower_only(a_ref[...], 0), pad], axis=0).T
    high, low = split2(v_one)
    v_high[...] = high
    v_low[...] = low
    cross = head[1, :, 0:256] - exact(hmat[ORDER:, :], htr[:, 0:256])
    f_rows = exact(cross, v_one)
    f_tr = jnp.concatenate([pad, f_rows], axis=0).T
    high, low = split2(f_tr)
    f_high[...] = high
    f_low[...] = low
    two = (head[1, :, 128:384] - exact(hmat[ORDER:, :], htr[:, 128:384])) - exact(f_rows, f_tr)
    a_ref[...] = jnp.where(lanes >= 64, two, 0.0)

    def first_of(start, count):
        rows = pl.ds(start, count)
        first = mul3(rbuf[rows, 0:256], v_high[...], v_low[...])
        rest = rbuf[rows, 128:384] - mul3(first, f_high[...], f_low[...])
        rbuf[rows, 0:128] = first[:, 0:128]
        spot = lax.broadcasted_iota(jnp.int32, (count, 128), 1)
        rbuf[rows, 128:256] = jnp.where(spot < 64, first[:, 128:256], rest[:, 0:128])
        rbuf[rows, 256:384] = rest[:, 128:256]
        squares[rows, :] = squares[rows, :] + (first[:, 0:128] * first[:, 0:128] + first[:, 128:256] * first[:, 128:256])

    def round_two(r, _):
        factor_round(a_ref, r, 64)
        first_of(pl.multiple_of(r * TILE, TILE), TILE)
        return 0

    lax.fori_loop(0, ROUNDS, round_two, 0)
    first_of(ROUNDS * TILE, LAST)

    v_two = jnp.concatenate([pad, lower_only(a_ref[...], 64)], axis=0).T
    high, low = split2(v_two)
    v_high[...] = high
    v_low[...] = low

    def send(start, count, n):
        rows = pl.ds(start, count)
        return pltpu.make_async_copy(rbuf.at[rows], out_hbm.at[rows], out_sem.at[n])

    def second_of(start, count, n, at):
        rows = pl.ds(start, count)
        second = mul3(rbuf[rows, 128:384], v_high[...], v_low[...])
        spot = lax.broadcasted_iota(jnp.int32, (count, 128), 1)
        rbuf[rows, 128:256] = jnp.where(spot < 64, rbuf[rows, 128:256], second[:, 0:128])
        rbuf[rows, 256:384] = second[:, 128:256]
        send(start, count, n).start()
        square = squares[rows, :] + (second[:, 0:128] * second[:, 0:128] + second[:, 128:256] * second[:, 128:256])
        ones = jnp.ones((8, 128), F32)
        total = lax.dot_general(ones, square, (((1,), (1,)), ((), ())), precision=HIGHEST, preferred_element_type=F32)
        for q in range(count // 128):
            sums[pl.ds(at + q, 1), :] = total[0:1, q * 128 : (q + 1) * 128]

    def round_three(r, _):
        second_of(pl.multiple_of(r * TILE, TILE), TILE, r, r * (TILE // 128))
        return 0

    lax.fori_loop(0, ROUNDS, round_three, 0)
    second_of(ROUNDS * TILE, LAST, ROUNDS, ROUNDS * TILE // 128)

    entry = lax.broadcasted_iota(jnp.int32, (38, 128), 0) * 128 + lax.broadcasted_iota(jnp.int32, (38, 128), 1)
    live = jnp.where(entry < alive, 1.0, 0.0)
    left = live * (diag_ref[...] - sums[...])
    top_left = jnp.max(left)
    top_diag = jnp.max(live * diag_ref[...])
    spot = lax.broadcasted_iota(jnp.int32, (1, 128), 1)
    top_ref[...] = jnp.where(spot < 64, top_left, top_diag)
    for n, (start, count) in enumerate(CHUNKS):
        send(start, count, n).wait()


def panels(everybody, pivots, live_blocks, diag, chol_done, new_cols):
    vmem = pl.BlockSpec(memory_space=pltpu.VMEM)
    hbm = pl.BlockSpec(memory_space=pl.ANY)
    return pl.pallas_call(
        panel_kernel,
        out_shape=(jax.ShapeDtypeStruct((ROWS, COLS), F32), jax.ShapeDtypeStruct((1, 128), F32)),
        in_specs=[vmem, vmem, pl.BlockSpec(memory_space=pltpu.SMEM), vmem, hbm, hbm],
        out_specs=(hbm, vmem),
        scratch_shapes=[
            pltpu.VMEM((ROWS, K), F32),
            pltpu.VMEM((ROWS, COLS), F32),
            pltpu.VMEM((ROWS, 128), F32),
            pltpu.VMEM((COLS, K), F32),
            pltpu.VMEM((K, COLS), F32),
            pltpu.VMEM((K, COLS), BF16),
            pltpu.VMEM((K, COLS), BF16),
            pltpu.VMEM((2, ORDER, COLS), F32),
            pltpu.VMEM((ORDER, 256), F32),
            pltpu.VMEM((256, 256), BF16),
            pltpu.VMEM((256, 256), BF16),
            pltpu.VMEM((256, 256), BF16),
            pltpu.VMEM((256, 256), BF16),
            pltpu.VMEM((38, 128), F32),
            pltpu.SemaphoreType.DMA((2, ROUNDS + 1)),
            pltpu.SemaphoreType.DMA((ROUNDS + 1,)),
        ],
        compiler_params=pltpu.CompilerParams(vmem_limit_bytes=VMEM_LIMIT),
    )(everybody, pivots, live_blocks, diag, chol_done, new_cols)


def top_kernel(in_ref, out_ref, table, own_sem, near_send, near_recv, far_send, far_recv):
    grp, blk = lax.axis_index("grp"), lax.axis_index("blk")
    barrier = pltpu.get_barrier_semaphore()
    near = [(lax.rem(grp + k, 8), blk) for k in range(1, 8)]
    far = [(grp, lax.rem(blk + k, 16)) for k in range(1, 16)]
    for there in near + far:
        pl.semaphore_signal(barrier, inc=1, device_id=there, device_id_type=MESH)
    mine = table.at[blk, grp]
    own = pltpu.make_async_copy(in_ref, mine, own_sem)
    own.start()
    pl.semaphore_wait(barrier, len(near) + len(far))
    one = []
    for n, there in enumerate(near):
        copy = pltpu.make_async_remote_copy(
            src_ref=in_ref, dst_ref=mine, send_sem=near_send.at[n], recv_sem=near_recv.at[n],
            device_id=there, device_id_type=MESH,
        )
        copy.start()
        one.append(copy)
    own.wait()
    for copy in one:
        copy.wait_recv()
    two = []
    for n, there in enumerate(far):
        copy = pltpu.make_async_remote_copy(
            src_ref=table.at[blk], dst_ref=table.at[blk], send_sem=far_send.at[n], recv_sem=far_recv.at[n],
            device_id=there, device_id_type=MESH,
        )
        copy.start()
        two.append(copy)
    for copy in two:
        copy.wait_recv()
    best = jnp.max(table[...].reshape(128, 128), axis=0, keepdims=True)
    spot = lax.broadcasted_iota(jnp.int32, (1, 128), 1)
    low = -3.0e38
    left = jnp.max(jnp.where(spot < 64, best, low), axis=1, keepdims=True)
    diag = jnp.max(jnp.where(spot < 64, low, best), axis=1, keepdims=True)
    out_ref[...] = jnp.broadcast_to(left / diag, (1, 128))
    for copy in one + two:
        copy.wait_send()


def top(mine):
    return pl.pallas_call(
        top_kernel,
        out_shape=jax.ShapeDtypeStruct((1, 128), F32),
        in_specs=[pl.BlockSpec(memory_space=pltpu.VMEM)],
        out_specs=pl.BlockSpec(memory_space=pltpu.VMEM),
        scratch_shapes=[
            pltpu.VMEM((16, 8, 1, 128), F32),
            pltpu.SemaphoreType.DMA,
            pltpu.SemaphoreType.DMA((7,)),
            pltpu.SemaphoreType.DMA((7,)),
            pltpu.SemaphoreType.DMA((15,)),
            pltpu.SemaphoreType.DMA((15,)),
        ],
        compiler_params=pltpu.CompilerParams(collective_id=1, has_side_effects=True),
    )(mine)


def body(chol_done, new_cols, diag_entries, pivots, live_blocks):
    slots = pick(pivots, chol_done, new_cols)
    everybody = gather(slots).reshape(128 * SLOT_ROWS, 128)
    diag = diag_entries.reshape(ROWS // 128, 128)
    vectors, mine = panels(everybody, pivots, live_blocks, diag, chol_done, new_cols)
    return vectors, top(mine)[0, 0:1]


def solution(mesh):
    placed = (P(("grp", "blk"), None), P(("grp", "blk"), None), P(("grp", "blk")), P(), P())
    return jax.shard_map(
        body, mesh=mesh, in_specs=placed, out_specs=(P(("grp", "blk"), None), P()), check_vma=False
    )
```

```python
import jax
import jax.numpy as jnp
from jax import lax
from jax.experimental import pallas as pl
from jax.experimental.pallas import tpu as pltpu
from jax.sharding import PartitionSpec as P

MESH = pl.DeviceIdType.MESH
HIGHEST = lax.Precision.HIGHEST
F32 = jnp.float32
BF16 = jnp.bfloat16
ROWS = 4864
K = 512
ORDER = 192
COLS = 384
BLOCK_ROWS = 256
SLOTS = 3
SLOT_ROWS = 40
STEP = 16
ROUNDS = ORDER // STEP
TILE = 384
LAST = ROWS - ROUNDS * TILE
CHUNKS = [(i * TILE, TILE) for i in range(ROUNDS)] + [(ROUNDS * TILE, LAST)]
BIG = 768
VMEM_LIMIT = 60 * 1024 * 1024
COLOURS = ((0, 16, "yxz"), (16, 16, "xzy"), (32, 8, "zyx"))


def slot_base(panel, slot):
    return slot * 6 if panel == 0 else 18 + slot * 7


def pick_kernel(piv_ref, chol_hbm, cols_hbm, out_ref, cbuf, nbuf, sem):
    me = lax.axis_index("grp") * 16 + lax.axis_index("blk")
    base = me * ROWS
    local = piv_ref[...] - base
    mine = (local >= 0) & (local < ROWS)
    spot = lax.broadcasted_iota(jnp.int32, (2, ORDER), 1)
    key = jnp.where(mine, (spot * 8192 + local).astype(F32), 4.0e6)
    found = []
    for slot in range(SLOTS):
        least = jnp.min(key, axis=1, keepdims=True)
        found.append(least)
        key = jnp.where(key <= least, 4.0e6, key)
    copies = []
    where_row = []
    for panel in range(2):
        for slot in range(SLOTS):
            value = found[slot][panel, 0].astype(jnp.int32)
            row = jnp.where(value < 4000000, value & 8191, 0)
            row = jnp.minimum(row, ROWS - 1)
            group = pl.multiple_of((row // 8) * 8, 8)
            n = panel * SLOTS + slot
            one = pltpu.make_async_copy(chol_hbm.at[pl.ds(group, 8)], cbuf.at[n], sem.at[0, n])
            two = pltpu.make_async_copy(cols_hbm.at[pl.ds(group, 8)], nbuf.at[n], sem.at[1, n])
            one.start()
            two.start()
            copies.append((one, two))
            where_row.append(row - group)
    for panel in range(2):
        for slot in range(SLOTS):
            n = panel * SLOTS + slot
            for copy in copies[n]:
                copy.wait()
            at = slot_base(panel, slot)
            sub = lax.broadcasted_iota(jnp.int32, (8, 128), 0) == where_row[n]
            for c in range(6 if panel == 0 else 7):
                tile = cbuf[n, :, c * 128 : c * 128 + 128] if c < 4 else nbuf[n, :, (c - 4) * 128 : (c - 3) * 128]
                out_ref[at + c : at + c + 1, :] = jnp.sum(jnp.where(sub, tile, 0.0), axis=0, keepdims=True)
    out_ref[39:40, :] = jnp.zeros((1, 128), F32)


def pick(pivots, chol_done, new_cols):
    return pl.pallas_call(
        pick_kernel,
        out_shape=jax.ShapeDtypeStruct((SLOT_ROWS, 128), F32),
        in_specs=[
            pl.BlockSpec(memory_space=pltpu.VMEM),
            pl.BlockSpec(memory_space=pl.ANY),
            pl.BlockSpec(memory_space=pl.ANY),
        ],
        out_specs=pl.BlockSpec(memory_space=pltpu.VMEM),
        scratch_shapes=[
            pltpu.VMEM((6, 8, K), F32),
            pltpu.VMEM((6, 8, COLS), F32),
            pltpu.SemaphoreType.DMA((2, 6)),
        ],
    )(pivots, chol_done, new_cols)


def gather_kernel(in_ref, g_ref, own_sem, send_sem, recv_sem, pass_send, pass_recv):
    grp, blk = lax.axis_index("grp"), lax.axis_index("blk")
    at = {"z": lax.div(grp, 2), "x": lax.div(blk, 4), "y": lax.rem(blk, 4)}
    core = lax.rem(grp, 2)

    def device(z, c, x, y):
        return (z * 2 + c, x * 4 + y)

    def beside(axis, k):
        there = dict(at)
        there[axis] = lax.rem(at[axis] + k, 4)
        return device(there["z"], core, there["x"], there["y"])

    partner = device(at["z"], 1 - core, at["x"], at["y"])
    barrier = pltpu.get_barrier_semaphore()
    for axis in "xyz":
        for k in (1, 2, 3):
            pl.semaphore_signal(barrier, inc=1, device_id=beside(axis, k), device_id_type=MESH)
    pl.semaphore_signal(barrier, inc=1, device_id=partner, device_id_type=MESH)
    own = pltpu.make_async_copy(in_ref, g_ref.at[at["z"], core, at["x"], at["y"]], own_sem)
    own.start()
    pl.semaphore_wait(barrier, 10)

    def region(colour, have, fixed):
        first, count, _ = COLOURS[colour]
        pick_at = [slice(None) if a in have else fixed[a] for a in "zxy"]
        return g_ref.at[pick_at[0], core, pick_at[1], pick_at[2], pl.ds(first, count), :]

    flights = {}

    def launch(colour, phase):
        first, count, order = COLOURS[colour]
        have = order[:phase]
        here = region(colour, have, at)
        for k in (2, 1, 3):
            source = in_ref.at[pl.ds(first, count), :] if phase == 0 else here
            copy = pltpu.make_async_remote_copy(
                src_ref=source,
                dst_ref=here,
                send_sem=send_sem.at[colour, phase, k - 1],
                recv_sem=recv_sem.at[colour, phase, k - 1],
                device_id=beside(order[phase], k),
                device_id_type=MESH,
            )
            copy.start()
            flights[colour, phase, k] = copy

    passes = []

    def hand_over(colour, piece, ref):
        copy = pltpu.make_async_remote_copy(
            src_ref=ref,
            dst_ref=ref,
            send_sem=pass_send.at[colour, piece],
            recv_sem=pass_recv.at[colour, piece],
            device_id=partner,
            device_id_type=MESH,
        )
        copy.start()
        passes.append(copy)

    colours = range(len(COLOURS))
    for colour in colours:
        launch(colour, 0)
    own.wait()
    for phase in (1, 2):
        for colour in colours:
            for k in (1, 3, 2):
                flights[colour, phase - 1, k].wait_recv()
            launch(colour, phase)
            if phase == 2:
                hand_over(colour, 0, region(colour, COLOURS[colour][2][:2], at))
    for k in (1, 3, 2):
        for colour in colours:
            flights[colour, 2, k].wait_recv()
            last = COLOURS[colour][2][2]
            there = dict(at)
            there[last] = lax.rem(at[last] + (4 - k), 4)
            hand_over(colour, k, region(colour, COLOURS[colour][2][:2], there))
    for copy in passes:
        copy.wait_recv()
    for copy in passes:
        copy.wait_send()
    for copy in flights.values():
        copy.wait_send()


def gather(slots):
    return pl.pallas_call(
        gather_kernel,
        out_shape=jax.ShapeDtypeStruct((4, 2, 4, 4, SLOT_ROWS, 128), F32),
        in_specs=[pl.BlockSpec(memory_space=pltpu.VMEM)],
        out_specs=pl.BlockSpec(memory_space=pltpu.VMEM),
        scratch_shapes=[
            pltpu.SemaphoreType.DMA,
            pltpu.SemaphoreType.DMA((3, 3, 3)),
            pltpu.SemaphoreType.DMA((3, 3, 3)),
            pltpu.SemaphoreType.DMA((3, 4)),
            pltpu.SemaphoreType.DMA((3, 4)),
        ],
        compiler_params=pltpu.CompilerParams(collective_id=0, has_side_effects=True),
    )(slots)


def split2(a):
    high = a.astype(BF16)
    return high, (a - high.astype(F32)).astype(BF16)


def split3(a):
    high = a.astype(BF16)
    rest = a - high.astype(F32)
    mid = rest.astype(BF16)
    return high, mid, (rest - mid.astype(F32)).astype(BF16)


def mul(a, b):
    return jnp.dot(a, b, preferred_element_type=F32)


def mul3(a, b_high, b_low):
    high, low = split2(a)
    return mul(high, b_high) + (mul(high, b_low) + mul(low, b_high))


def exact(a, b):
    return jnp.dot(a, b, precision=HIGHEST, preferred_element_type=F32)


def over_lanes(x, lane):
    return jnp.take_along_axis(x, jnp.full((8, 128), lane, jnp.int32), axis=1)


def over_rows(x, row):
    return jnp.broadcast_to(x[row : row + 1, :], (8, 128))


def factor_round(a_ref, r, off):
    rs = pl.multiple_of(r * STEP, STEP)
    c0 = off + r * STEP
    t = c0 // 128
    l0 = c0 - t * 128
    tl = pl.multiple_of(t * 128, 128)
    lane = lax.broadcasted_iota(jnp.int32, (8, 128), 1)
    sub = lax.broadcasted_iota(jnp.int32, (8, 128), 0)
    raw = [a_ref[pl.ds(rs + 8 * q, 8), pl.ds(tl, 128)] for q in range(2)]
    col = {}
    for j in range(STEP):
        for q in range(j // 8, 2):
            col[j, q] = over_lanes(raw[q], l0 + j)
    row = {}
    for q in range(2):
        for h in range(2):
            x = a_ref[pl.ds(rs + 8 * q, 8), h * 128 : (h + 1) * 128]
            rel = lane + (h * 128) - c0
            unit = jnp.where(rel == sub + 8 * q, 1.0, 0.0)
            row[q, h] = jnp.where((rel >= 0) & (rel < STEP), unit, x)
    for j in range(STEP):
        jq, js = j // 8, j % 8
        scale = lax.rsqrt(over_rows(col[j, jq], js))
        low = {q: col[j, q] * scale for q in range(jq, 2)}
        for m in range(j + 1, STEP):
            times = over_rows(low[m // 8], m % 8)
            for q in range(m // 8, 2):
                col[m, q] = col[m, q] - low[q] * times
        low[jq] = jnp.where(sub > js, low[jq], 0.0)
        for h in range(2):
            lead = over_rows(row[jq, h], js) * scale
            for q in range(jq, 2):
                row[q, h] = row[q, h] - low[q] * lead
            row[jq, h] = jnp.where(sub == js, lead, row[jq, h])
    for q in range(2):
        for h in range(2):
            a_ref[pl.ds(rs + 8 * q, 8), h * 128 : (h + 1) * 128] = row[q, h]
    u = jnp.concatenate([jnp.concatenate([row[q, h] for h in range(2)], axis=1) for q in range(2)], axis=0)
    lanes = lax.broadcasted_iota(jnp.int32, (STEP, 256), 1)
    high, mid, low3 = split3(u)
    zero = jnp.zeros_like(u)
    ahead = lanes >= c0 + STEP
    h_l, m_l, l_l = split3(jnp.where(ahead, u, zero))
    left = jnp.concatenate([h_l, h_l, m_l, m_l, h_l, l_l], axis=0)
    right = jnp.concatenate([high, mid, high, mid, low3, high], axis=0)
    z = lax.dot_general(left, right, (((0,), (0,)), ((), ())), preferred_element_type=F32)
    rows_i = lax.broadcasted_iota(jnp.int32, (ORDER, 256), 0)
    cols_i = lax.broadcasted_iota(jnp.int32, (ORDER, 256), 1)
    old = (rows_i >= rs + STEP) & (cols_i >= c0) & (cols_i < c0 + STEP)
    a_ref[...] = jnp.where(old, 0.0, a_ref[...]) - z[off : off + ORDER, :]


def lower_only(a, off):
    row = lax.broadcasted_iota(jnp.int32, (ORDER, 256), 0)
    col = lax.broadcasted_iota(jnp.int32, (ORDER, 256), 1) - off
    return jnp.where((col >= 0) & (col <= row), a, 0.0)


def panel_kernel(g_ref, piv_ref, live_ref, diag_ref, chol_hbm, cols_hbm, out_hbm, top_ref,
                 chol, rbuf, squares, hmat, htr, ht_high, ht_low, head, a_ref,
                 v_high, v_low, w_high, w_low, sums, in_sem, out_sem):
    me = lax.axis_index("grp") * 16 + lax.axis_index("blk")
    alive = live_ref[me] * BLOCK_ROWS

    def fetch(start, count, n):
        rows = pl.ds(start, count)
        return (
            pltpu.make_async_copy(chol_hbm.at[rows], chol.at[rows], in_sem.at[0, n]),
            pltpu.make_async_copy(cols_hbm.at[rows], rbuf.at[rows], in_sem.at[1, n]),
        )

    for n, (start, count) in enumerate(CHUNKS):
        for copy in fetch(start, count, n):
            copy.start()

    q_i = lax.broadcasted_iota(jnp.int32, (ORDER, ORDER), 1)
    p_i = lax.broadcasted_iota(jnp.int32, (ORDER, ORDER), 0)
    for panel in range(2):
        owner_row = (piv_ref[panel : panel + 1, :] // ROWS).astype(F32)
        owner_all = jnp.broadcast_to(owner_row, (ORDER, ORDER))
        owner = jnp.sum(jnp.where(q_i == p_i, owner_all, 0.0), axis=1, keepdims=True)
        before = (owner_all == owner) & (q_i < p_i)
        rank = jnp.sum(jnp.where(before, 1.0, 0.0), axis=1, keepdims=True)
        dev = lax.broadcasted_iota(jnp.int32, (ORDER, 128), 1).astype(F32)
        hot = jnp.concatenate(
            [jnp.where((dev == owner) & (rank == float(s)), 1.0, 0.0) for s in range(SLOTS)], axis=1
        ).astype(BF16)
        for c in range(6 if panel == 0 else 7):
            pieces = [g_ref[pl.ds(slot_base(panel, s) + c, 128, stride=SLOT_ROWS), :] for s in range(SLOTS)]
            high, mid, low = split3(jnp.concatenate(pieces, axis=0))
            rows = mul(hot, high) + (mul(hot, mid) + mul(hot, low))
            if c < 4:
                hmat[panel * ORDER : (panel + 1) * ORDER, c * 128 : (c + 1) * 128] = rows
            else:
                head[panel, :, (c - 4) * 128 : (c - 3) * 128] = rows
    htr[...] = hmat[...].T
    high, low = split2(htr[...])
    ht_high[...] = high
    ht_low[...] = low

    lanes = lax.broadcasted_iota(jnp.int32, (ORDER, 256), 1)
    one = head[0, :, 0:256] - exact(hmat[0:ORDER, :], htr[:, 0:256])
    a_ref[...] = jnp.where(lanes < ORDER, one, 0.0)

    def residual(start, count):
        rows = pl.ds(start, count)
        tile = chol[rows, :]
        left = rbuf[rows, :] - mul3(tile, ht_high[...], ht_low[...])
        spot = lax.broadcasted_iota(jnp.int32, (count, COLS), 0) + start
        rbuf[rows, :] = jnp.where(spot < alive, left, 0.0)
        square = tile * tile
        squares[rows, :] = (square[:, 0:128] + square[:, 128:256]) + (square[:, 256:384] + square[:, 384:512])

    def round_one(r, _):
        start = pl.multiple_of(r * TILE, TILE)
        for copy in fetch(start, TILE, r):
            copy.wait()
        residual(start, TILE)
        factor_round(a_ref, r, 0)
        return 0

    lax.fori_loop(0, ROUNDS, round_one, 0)
    for copy in fetch(ROUNDS * TILE, LAST, ROUNDS):
        copy.wait()
    residual(ROUNDS * TILE, LAST)

    pad = jnp.zeros((64, 256), F32)
    v_one = jnp.concatenate([lower_only(a_ref[...], 0), pad], axis=0).T
    cross = head[1, :, 0:256] - exact(hmat[ORDER:, :], htr[:, 0:256])
    f_rows = exact(cross, v_one)
    f_tr = jnp.concatenate([pad, f_rows], axis=0).T
    high, low = split2(jnp.concatenate([v_one, exact(v_one, f_tr)], axis=1))
    w_high[...] = high
    w_low[...] = low
    two = (head[1, :, 128:384] - exact(hmat[ORDER:, :], htr[:, 128:384])) - exact(f_rows, f_tr)
    a_ref[...] = jnp.where(lanes >= 64, two, 0.0)

    def first_of(start, count):
        rows = pl.ds(start, count)
        both = mul3(rbuf[rows, 0:256], w_high[...], w_low[...])
        first = both[:, 0:256]
        rest = rbuf[rows, 128:384] - both[:, 256:512]
        rbuf[rows, 0:128] = first[:, 0:128]
        spot = lax.broadcasted_iota(jnp.int32, (count, 128), 1)
        rbuf[rows, 128:256] = jnp.where(spot < 64, first[:, 128:256], rest[:, 0:128])
        rbuf[rows, 256:384] = rest[:, 128:256]
        squares[rows, :] = squares[rows, :] + (first[:, 0:128] * first[:, 0:128] + first[:, 128:256] * first[:, 128:256])

    def round_two(r, _):
        first_of(pl.multiple_of(r * TILE, TILE), TILE)
        factor_round(a_ref, r, 64)
        return 0

    lax.fori_loop(0, ROUNDS, round_two, 0)
    first_of(ROUNDS * TILE, LAST)

    v_two = jnp.concatenate([pad, lower_only(a_ref[...], 64)], axis=0).T
    high, low = split2(v_two)
    v_high[...] = high
    v_low[...] = low

    def send(start, count, n):
        rows = pl.ds(start, count)
        return pltpu.make_async_copy(rbuf.at[rows], out_hbm.at[rows], out_sem.at[n])

    def second_of(start, count, n, at):
        rows = pl.ds(start, count)
        second = mul3(rbuf[rows, 128:384], v_high[...], v_low[...])
        spot = lax.broadcasted_iota(jnp.int32, (count, 128), 1)
        rbuf[rows, 128:256] = jnp.where(spot < 64, rbuf[rows, 128:256], second[:, 0:128])
        rbuf[rows, 256:384] = second[:, 128:256]
        send(start, count, n).start()
        square = squares[rows, :] + (second[:, 0:128] * second[:, 0:128] + second[:, 128:256] * second[:, 128:256])
        for q in range(count // 128):
            turned = square[q * 128 : (q + 1) * 128, :].T
            sums[pl.ds(at + q, 1), :] = jnp.sum(turned, axis=0, keepdims=True)

    def round_three(r, _):
        second_of(pl.multiple_of(r * BIG, BIG), BIG, r, r * (BIG // 128))
        return 0

    lax.fori_loop(0, ROWS // BIG, round_three, 0)
    second_of(ROWS // BIG * BIG, ROWS % BIG, ROWS // BIG, ROWS // BIG * BIG // 128)

    entry = lax.broadcasted_iota(jnp.int32, (38, 128), 0) * 128 + lax.broadcasted_iota(jnp.int32, (38, 128), 1)
    live = jnp.where(entry < alive, 1.0, 0.0)
    left = live * (diag_ref[...] - sums[...])
    top_left = jnp.max(left)
    top_diag = jnp.max(live * diag_ref[...])
    spot = lax.broadcasted_iota(jnp.int32, (1, 128), 1)
    top_ref[...] = jnp.where(spot < 64, top_left, top_diag)
    for n in range(ROWS // BIG):
        send(n * BIG, BIG, n).wait()
    send(ROWS // BIG * BIG, ROWS % BIG, ROWS // BIG).wait()


def panels(everybody, pivots, live_blocks, diag, chol_done, new_cols):
    vmem = pl.BlockSpec(memory_space=pltpu.VMEM)
    hbm = pl.BlockSpec(memory_space=pl.ANY)
    return pl.pallas_call(
        panel_kernel,
        out_shape=(jax.ShapeDtypeStruct((ROWS, COLS), F32), jax.ShapeDtypeStruct((1, 128), F32)),
        in_specs=[vmem, vmem, pl.BlockSpec(memory_space=pltpu.SMEM), vmem, hbm, hbm],
        out_specs=(hbm, vmem),
        scratch_shapes=[
            pltpu.VMEM((ROWS, K), F32),
            pltpu.VMEM((ROWS, COLS), F32),
            pltpu.VMEM((ROWS, 128), F32),
            pltpu.VMEM((COLS, K), F32),
            pltpu.VMEM((K, COLS), F32),
            pltpu.VMEM((K, COLS), BF16),
            pltpu.VMEM((K, COLS), BF16),
            pltpu.VMEM((2, ORDER, COLS), F32),
            pltpu.VMEM((ORDER, 256), F32),
            pltpu.VMEM((256, 256), BF16),
            pltpu.VMEM((256, 256), BF16),
            pltpu.VMEM((256, 512), BF16),
            pltpu.VMEM((256, 512), BF16),
            pltpu.VMEM((38, 128), F32),
            pltpu.SemaphoreType.DMA((2, ROUNDS + 1)),
            pltpu.SemaphoreType.DMA((ROUNDS + 1,)),
        ],
        compiler_params=pltpu.CompilerParams(vmem_limit_bytes=VMEM_LIMIT),
    )(everybody, pivots, live_blocks, diag, chol_done, new_cols)


def top_kernel(in_ref, out_ref, table, own_sem, near_send, near_recv, far_send, far_recv):
    grp, blk = lax.axis_index("grp"), lax.axis_index("blk")
    barrier = pltpu.get_barrier_semaphore()
    near = [(lax.rem(grp + k, 8), blk) for k in range(1, 8)]
    far = [(grp, lax.rem(blk + k, 16)) for k in range(1, 16)]
    for there in near + far:
        pl.semaphore_signal(barrier, inc=1, device_id=there, device_id_type=MESH)
    mine = table.at[blk, grp]
    own = pltpu.make_async_copy(in_ref, mine, own_sem)
    own.start()
    pl.semaphore_wait(barrier, len(near) + len(far))
    one = []
    for n, there in enumerate(near):
        copy = pltpu.make_async_remote_copy(
            src_ref=in_ref, dst_ref=mine, send_sem=near_send.at[n], recv_sem=near_recv.at[n],
            device_id=there, device_id_type=MESH,
        )
        copy.start()
        one.append(copy)
    own.wait()
    for copy in one:
        copy.wait_recv()
    two = []
    for n, there in enumerate(far):
        copy = pltpu.make_async_remote_copy(
            src_ref=table.at[blk], dst_ref=table.at[blk], send_sem=far_send.at[n], recv_sem=far_recv.at[n],
            device_id=there, device_id_type=MESH,
        )
        copy.start()
        two.append(copy)
    for copy in two:
        copy.wait_recv()
    best = jnp.max(table[...].reshape(128, 128), axis=0, keepdims=True)
    spot = lax.broadcasted_iota(jnp.int32, (1, 128), 1)
    low = -3.0e38
    left = jnp.max(jnp.where(spot < 64, best, low), axis=1, keepdims=True)
    diag = jnp.max(jnp.where(spot < 64, low, best), axis=1, keepdims=True)
    out_ref[...] = jnp.broadcast_to(left / diag, (1, 128))
    for copy in one + two:
        copy.wait_send()


def top(mine):
    return pl.pallas_call(
        top_kernel,
        out_shape=jax.ShapeDtypeStruct((1, 128), F32),
        in_specs=[pl.BlockSpec(memory_space=pltpu.VMEM)],
        out_specs=pl.BlockSpec(memory_space=pltpu.VMEM),
        scratch_shapes=[
            pltpu.VMEM((16, 8, 1, 128), F32),
            pltpu.SemaphoreType.DMA,
            pltpu.SemaphoreType.DMA((7,)),
            pltpu.SemaphoreType.DMA((7,)),
            pltpu.SemaphoreType.DMA((15,)),
            pltpu.SemaphoreType.DMA((15,)),
        ],
        compiler_params=pltpu.CompilerParams(collective_id=1, has_side_effects=True),
    )(mine)


def body(chol_done, new_cols, diag_entries, pivots, live_blocks):
    slots = pick(pivots, chol_done, new_cols)
    everybody = gather(slots).reshape(128 * SLOT_ROWS, 128)
    diag = diag_entries.reshape(ROWS // 128, 128)
    vectors, mine = panels(everybody, pivots, live_blocks, diag, chol_done, new_cols)
    return vectors, top(mine)[0, 0:1]


def solution(mesh):
    placed = (P(("grp", "blk"), None), P(("grp", "blk"), None), P(("grp", "blk")), P(), P())
    return jax.shard_map(
        body, mesh=mesh, in_specs=placed, out_specs=(P(("grp", "blk"), None), P()), check_vma=False
    )
```

```python
import jax
import jax.numpy as jnp
from jax import lax
from jax.experimental import pallas as pl
from jax.experimental.pallas import tpu as pltpu
from jax.sharding import PartitionSpec as P

MESH = pl.DeviceIdType.MESH
HIGHEST = lax.Precision.HIGHEST
F32 = jnp.float32
BF16 = jnp.bfloat16
ROWS = 4864
K = 512
ORDER = 192
COLS = 384
BLOCK_ROWS = 256
SLOTS = 3
SLOT_ROWS = 40
STEP = 16
ROUNDS = ORDER // STEP
BIG = 768
TILE = 384
CHUNKS = [(i * BIG, BIG) for i in range(ROWS // BIG)] + [(ROWS // BIG * BIG, ROWS % BIG)]
VMEM_LIMIT = 24 * 1024 * 1024
COLOURS = ((0, 16, "yxz"), (16, 16, "xzy"), (32, 8, "zyx"))


def slot_base(panel, slot):
    return slot * 6 if panel == 0 else 18 + slot * 7


def pick_kernel(piv_ref, chol_hbm, cols_hbm, out_ref, cbuf, nbuf, sem):
    me = lax.axis_index("grp") * 16 + lax.axis_index("blk")
    base = me * ROWS
    local = piv_ref[...] - base
    mine = (local >= 0) & (local < ROWS)
    spot = lax.broadcasted_iota(jnp.int32, (2, ORDER), 1)
    key = jnp.where(mine, (spot * 8192 + local).astype(F32), 4.0e6)
    found = []
    for slot in range(SLOTS):
        least = jnp.min(key, axis=1, keepdims=True)
        found.append(least)
        key = jnp.where(key <= least, 4.0e6, key)
    copies = []
    where_row = []
    for panel in range(2):
        for slot in range(SLOTS):
            value = found[slot][panel, 0].astype(jnp.int32)
            row = jnp.where(value < 4000000, value & 8191, 0)
            row = jnp.minimum(row, ROWS - 1)
            group = pl.multiple_of((row // 8) * 8, 8)
            n = panel * SLOTS + slot
            one = pltpu.make_async_copy(chol_hbm.at[pl.ds(group, 8)], cbuf.at[n], sem.at[0, n])
            two = pltpu.make_async_copy(cols_hbm.at[pl.ds(group, 8)], nbuf.at[n], sem.at[1, n])
            one.start()
            two.start()
            copies.append((one, two))
            where_row.append(row - group)
    for panel in range(2):
        for slot in range(SLOTS):
            n = panel * SLOTS + slot
            for copy in copies[n]:
                copy.wait()
            at = slot_base(panel, slot)
            sub = lax.broadcasted_iota(jnp.int32, (8, 128), 0) == where_row[n]
            for c in range(6 if panel == 0 else 7):
                tile = cbuf[n, :, c * 128 : c * 128 + 128] if c < 4 else nbuf[n, :, (c - 4) * 128 : (c - 3) * 128]
                out_ref[at + c : at + c + 1, :] = jnp.sum(jnp.where(sub, tile, 0.0), axis=0, keepdims=True)
    out_ref[39:40, :] = jnp.zeros((1, 128), F32)


def pick(pivots, chol_done, new_cols):
    return pl.pallas_call(
        pick_kernel,
        out_shape=jax.ShapeDtypeStruct((SLOT_ROWS, 128), F32),
        in_specs=[
            pl.BlockSpec(memory_space=pltpu.VMEM),
            pl.BlockSpec(memory_space=pltpu.HBM),
            pl.BlockSpec(memory_space=pltpu.HBM),
        ],
        out_specs=pl.BlockSpec(memory_space=pltpu.VMEM),
        scratch_shapes=[
            pltpu.VMEM((6, 8, K), F32),
            pltpu.VMEM((6, 8, COLS), F32),
            pltpu.SemaphoreType.DMA((2, 6)),
        ],
        compiler_params=pltpu.CompilerParams(vmem_limit_bytes=60 * 1024 * 1024),
    )(pivots, chol_done, new_cols)


def gather_kernel(in_ref, g_ref, own_sem, send_sem, recv_sem, pass_send, pass_recv):
    grp, blk = lax.axis_index("grp"), lax.axis_index("blk")
    at = {"z": lax.div(grp, 2), "x": lax.div(blk, 4), "y": lax.rem(blk, 4)}
    core = lax.rem(grp, 2)

    def device(z, c, x, y):
        return (z * 2 + c, x * 4 + y)

    def beside(axis, k):
        there = dict(at)
        there[axis] = lax.rem(at[axis] + k, 4)
        return device(there["z"], core, there["x"], there["y"])

    partner = device(at["z"], 1 - core, at["x"], at["y"])
    barrier = pltpu.get_barrier_semaphore()
    for axis in "xyz":
        for k in (1, 2, 3):
            pl.semaphore_signal(barrier, inc=1, device_id=beside(axis, k), device_id_type=MESH)
    pl.semaphore_signal(barrier, inc=1, device_id=partner, device_id_type=MESH)
    own = pltpu.make_async_copy(in_ref, g_ref.at[at["z"], core, at["x"], at["y"]], own_sem)
    own.start()
    pl.semaphore_wait(barrier, 10)

    def region(colour, have, fixed):
        first, count, _ = COLOURS[colour]
        pick_at = [slice(None) if a in have else fixed[a] for a in "zxy"]
        return g_ref.at[pick_at[0], core, pick_at[1], pick_at[2], pl.ds(first, count), :]

    flights = {}

    def launch(colour, phase):
        first, count, order = COLOURS[colour]
        have = order[:phase]
        here = region(colour, have, at)
        for k in (2, 1, 3):
            source = in_ref.at[pl.ds(first, count), :] if phase == 0 else here
            copy = pltpu.make_async_remote_copy(
                src_ref=source,
                dst_ref=here,
                send_sem=send_sem.at[colour, phase, k - 1],
                recv_sem=recv_sem.at[colour, phase, k - 1],
                device_id=beside(order[phase], k),
                device_id_type=MESH,
            )
            copy.start()
            flights[colour, phase, k] = copy

    passes = []

    def hand_over(colour, piece, ref):
        copy = pltpu.make_async_remote_copy(
            src_ref=ref,
            dst_ref=ref,
            send_sem=pass_send.at[colour, piece],
            recv_sem=pass_recv.at[colour, piece],
            device_id=partner,
            device_id_type=MESH,
        )
        copy.start()
        passes.append(copy)

    colours = range(len(COLOURS))
    for colour in colours:
        launch(colour, 0)
    own.wait()
    for phase in (1, 2):
        for colour in colours:
            for k in (1, 3, 2):
                flights[colour, phase - 1, k].wait_recv()
            launch(colour, phase)
            if phase == 2:
                hand_over(colour, 0, region(colour, COLOURS[colour][2][:2], at))
    for k in (1, 3, 2):
        for colour in colours:
            flights[colour, 2, k].wait_recv()
            last = COLOURS[colour][2][2]
            there = dict(at)
            there[last] = lax.rem(at[last] + (4 - k), 4)
            hand_over(colour, k, region(colour, COLOURS[colour][2][:2], there))
    for copy in passes:
        copy.wait_recv()
    for copy in passes:
        copy.wait_send()
    for copy in flights.values():
        copy.wait_send()


def gather(slots):
    return pl.pallas_call(
        gather_kernel,
        out_shape=jax.ShapeDtypeStruct((4, 2, 4, 4, SLOT_ROWS, 128), F32),
        in_specs=[pl.BlockSpec(memory_space=pltpu.VMEM)],
        out_specs=pl.BlockSpec(memory_space=pltpu.VMEM),
        scratch_shapes=[
            pltpu.SemaphoreType.DMA,
            pltpu.SemaphoreType.DMA((3, 3, 3)),
            pltpu.SemaphoreType.DMA((3, 3, 3)),
            pltpu.SemaphoreType.DMA((3, 4)),
            pltpu.SemaphoreType.DMA((3, 4)),
        ],
        compiler_params=pltpu.CompilerParams(collective_id=0, has_side_effects=True, vmem_limit_bytes=4 * 1024 * 1024),
        cost_estimate=pl.CostEstimate(flops=20_000_000_000, bytes_accessed=2_700_000, transcendentals=0),
    )(slots)


def split2(a):
    high = a.astype(BF16)
    return high, (a - high.astype(F32)).astype(BF16)


def split3(a):
    high = a.astype(BF16)
    rest = a - high.astype(F32)
    mid = rest.astype(BF16)
    return high, mid, (rest - mid.astype(F32)).astype(BF16)


def mul(a, b):
    return jnp.dot(a, b, preferred_element_type=F32)


def mul3(a, b_high, b_low):
    high, low = split2(a)
    return mul(high, b_high) + (mul(high, b_low) + mul(low, b_high))


def exact(a, b):
    return jnp.dot(a, b, precision=HIGHEST, preferred_element_type=F32)


def over_lanes(x, lane):
    return jnp.take_along_axis(x, jnp.full((8, 128), lane, jnp.int32), axis=1)


def over_rows(x, row):
    return jnp.broadcast_to(x[row : row + 1, :], (8, 128))


def factor_round(a_ref, r, off):
    rs = pl.multiple_of(r * STEP, STEP)
    c0 = off + r * STEP
    t = c0 // 128
    l0 = c0 - t * 128
    tl = pl.multiple_of(t * 128, 128)
    lane = lax.broadcasted_iota(jnp.int32, (8, 128), 1)
    sub = lax.broadcasted_iota(jnp.int32, (8, 128), 0)
    raw = [a_ref[pl.ds(rs + 8 * q, 8), pl.ds(tl, 128)] for q in range(2)]
    col = {}
    for j in range(STEP):
        for q in range(j // 8, 2):
            col[j, q] = over_lanes(raw[q], l0 + j)
    row = {}
    for q in range(2):
        for h in range(2):
            x = a_ref[pl.ds(rs + 8 * q, 8), h * 128 : (h + 1) * 128]
            rel = lane + (h * 128) - c0
            unit = jnp.where(rel == sub + 8 * q, 1.0, 0.0)
            row[q, h] = jnp.where((rel >= 0) & (rel < STEP), unit, x)
    for j in range(STEP):
        jq, js = j // 8, j % 8
        scale = lax.rsqrt(over_rows(col[j, jq], js))
        low = {q: col[j, q] * scale for q in range(jq, 2)}
        for m in range(j + 1, STEP):
            times = over_rows(low[m // 8], m % 8)
            for q in range(m // 8, 2):
                col[m, q] = col[m, q] - low[q] * times
        low[jq] = jnp.where(sub > js, low[jq], 0.0)
        for h in range(2):
            lead = over_rows(row[jq, h], js) * scale
            for q in range(jq, 2):
                row[q, h] = row[q, h] - low[q] * lead
            row[jq, h] = jnp.where(sub == js, lead, row[jq, h])
    for q in range(2):
        for h in range(2):
            a_ref[pl.ds(rs + 8 * q, 8), h * 128 : (h + 1) * 128] = row[q, h]
    u = jnp.concatenate([jnp.concatenate([row[q, h] for h in range(2)], axis=1) for q in range(2)], axis=0)
    lanes = lax.broadcasted_iota(jnp.int32, (STEP, 256), 1)
    high, mid, low3 = split3(u)
    zero = jnp.zeros_like(u)
    ahead = lanes >= c0 + STEP
    h_l, m_l, l_l = split3(jnp.where(ahead, u, zero))
    left = jnp.concatenate([h_l, h_l, m_l, m_l, h_l, l_l], axis=0)
    right = jnp.concatenate([high, mid, high, mid, low3, high], axis=0)
    z = lax.dot_general(left, right, (((0,), (0,)), ((), ())), preferred_element_type=F32)
    rows_i = lax.broadcasted_iota(jnp.int32, (ORDER, 256), 0)
    cols_i = lax.broadcasted_iota(jnp.int32, (ORDER, 256), 1)
    old = (rows_i >= rs + STEP) & (cols_i >= c0) & (cols_i < c0 + STEP)
    a_ref[...] = jnp.where(old, 0.0, a_ref[...]) - z[off : off + ORDER, :]


def lower_only(a, off):
    row = lax.broadcasted_iota(jnp.int32, (ORDER, 256), 0)
    col = lax.broadcasted_iota(jnp.int32, (ORDER, 256), 1) - off
    return jnp.where((col >= 0) & (col <= row), a, 0.0)


def panel_kernel(g_ref, piv_ref, live_ref, diag_ref, chol, cols, out_hbm, top_ref,
                 rbuf, squares, hmat, htr, ht_pair, head, a_ref,
                 v_high, v_low, w_pair, sums, out_sem):
    me = lax.axis_index("grp") * 16 + lax.axis_index("blk")
    alive = live_ref[me] * BLOCK_ROWS

    q_i = lax.broadcasted_iota(jnp.int32, (ORDER, ORDER), 1)
    p_i = lax.broadcasted_iota(jnp.int32, (ORDER, ORDER), 0)
    for panel in range(2):
        owner_row = (piv_ref[panel : panel + 1, :] // ROWS).astype(F32)
        owner_all = jnp.broadcast_to(owner_row, (ORDER, ORDER))
        owner = jnp.sum(jnp.where(q_i == p_i, owner_all, 0.0), axis=1, keepdims=True)
        before = (owner_all == owner) & (q_i < p_i)
        rank = jnp.sum(jnp.where(before, 1.0, 0.0), axis=1, keepdims=True)
        dev = lax.broadcasted_iota(jnp.int32, (ORDER, 128), 1).astype(F32)
        hot = jnp.concatenate(
            [jnp.where((dev == owner) & (rank == float(s)), 1.0, 0.0) for s in range(SLOTS)], axis=1
        ).astype(BF16)
        for c in range(6 if panel == 0 else 7):
            pieces = [g_ref[pl.ds(slot_base(panel, s) + c, 128, stride=SLOT_ROWS), :] for s in range(SLOTS)]
            high, mid, low = split3(jnp.concatenate(pieces, axis=0))
            rows = mul(hot, high) + (mul(hot, mid) + mul(hot, low))
            if c < 4:
                hmat[panel * ORDER : (panel + 1) * ORDER, c * 128 : (c + 1) * 128] = rows
            else:
                head[panel, :, (c - 4) * 128 : (c - 3) * 128] = rows
    htr[...] = hmat[...].T
    lanes = lax.broadcasted_iota(jnp.int32, (ORDER, 256), 1)
    one = head[0, :, 0:256] - exact(hmat[0:ORDER, :], htr[:, 0:256])
    a_ref[...] = jnp.where(lanes < ORDER, one, 0.0)
    head[1, :, :] = head[1, :, :] - exact(hmat[ORDER:, :], htr[...])
    high, low = split2(htr[...])
    ht_pair[:, 0:COLS] = high
    ht_pair[:, COLS:] = low

    def residual_high(start, count):
        rows = pl.ds(start, count)
        both = mul(chol[rows, :].astype(BF16), ht_pair[...])
        rbuf[rows, :] = cols[rows, :] - (both[:, 0:COLS] + both[:, COLS:])

    def residual_low(start, count):
        rows = pl.ds(start, count)
        tile = chol[rows, :]
        left = rbuf[rows, :] - mul(split2(tile)[1], ht_pair[:, 0:COLS])
        spot = lax.broadcasted_iota(jnp.int32, (count, COLS), 0) + start
        rbuf[rows, :] = jnp.where(spot < alive, left, 0.0)
        square = tile * tile
        squares[rows, :] = (square[:, 0:128] + square[:, 128:256]) + (square[:, 256:384] + square[:, 384:512])

    def round_one(r, _):
        start = pl.multiple_of(r * BIG, BIG)
        residual_high(start, BIG)
        factor_round(a_ref, 2 * r, 0)
        residual_low(start, BIG)
        factor_round(a_ref, 2 * r + 1, 0)
        return 0

    lax.fori_loop(0, ROUNDS // 2, round_one, 0)
    residual_high(*CHUNKS[-1])
    residual_low(*CHUNKS[-1])

    pad = jnp.zeros((64, 256), F32)
    v_one = jnp.concatenate([lower_only(a_ref[...], 0), pad], axis=0).T
    f_rows = exact(head[1, :, 0:256], v_one)
    f_tr = jnp.concatenate([pad, f_rows], axis=0).T
    two = head[1, :, 128:384] - exact(f_rows, f_tr)
    a_ref[...] = jnp.where(lanes >= 64, two, 0.0)
    high, low = split2(jnp.concatenate([v_one, exact(v_one, f_tr)], axis=1))
    w_pair[:, 0:512] = high
    w_pair[:, 512:] = low

    def first_of(start, count):
        rows = pl.ds(start, count)
        high, low = split2(rbuf[rows, 0:256])
        wide = mul(high, w_pair[...])
        both = (wide[:, 0:512] + wide[:, 512:]) + mul(low, w_pair[:, 0:512])
        first = both[:, 0:256]
        rest = rbuf[rows, 128:384] - both[:, 256:512]
        rbuf[rows, 0:128] = first[:, 0:128]
        spot = lax.broadcasted_iota(jnp.int32, (count, 128), 1)
        rbuf[rows, 128:256] = jnp.where(spot < 64, first[:, 128:256], rest[:, 0:128])
        rbuf[rows, 256:384] = rest[:, 128:256]
        squares[rows, :] = squares[rows, :] + (first[:, 0:128] * first[:, 0:128] + first[:, 128:256] * first[:, 128:256])

    def round_two(r, _):
        first_of(pl.multiple_of(r * TILE, TILE), TILE)
        factor_round(a_ref, r, 64)
        return 0

    lax.fori_loop(0, ROUNDS, round_two, 0)
    first_of(*CHUNKS[-1])

    v_two = jnp.concatenate([pad, lower_only(a_ref[...], 64)], axis=0).T
    high, low = split2(v_two)
    v_high[...] = high
    v_low[...] = low

    def send(start, count, n):
        rows = pl.ds(start, count)
        return pltpu.make_async_copy(rbuf.at[rows], out_hbm.at[rows], out_sem.at[n])

    def second_of(start, count, n, at):
        rows = pl.ds(start, count)
        second = mul3(rbuf[rows, 128:384], v_high[...], v_low[...])
        spot = lax.broadcasted_iota(jnp.int32, (count, 128), 1)
        rbuf[rows, 128:256] = jnp.where(spot < 64, rbuf[rows, 128:256], second[:, 0:128])
        rbuf[rows, 256:384] = second[:, 128:256]
        send(start, count, n).start()
        square = squares[rows, :] + (second[:, 0:128] * second[:, 0:128] + second[:, 128:256] * second[:, 128:256])
        for q in range(count // 128):
            turned = square[q * 128 : (q + 1) * 128, :].T
            sums[pl.ds(at + q, 1), :] = jnp.sum(turned, axis=0, keepdims=True)

    def round_three(r, _):
        second_of(pl.multiple_of(r * BIG, BIG), BIG, r, r * (BIG // 128))
        return 0

    lax.fori_loop(0, ROWS // BIG, round_three, 0)
    second_of(*CHUNKS[-1], len(CHUNKS) - 1, CHUNKS[-1][0] // 128)

    entry = lax.broadcasted_iota(jnp.int32, (38, 128), 0) * 128 + lax.broadcasted_iota(jnp.int32, (38, 128), 1)
    live = jnp.where(entry < alive, 1.0, 0.0)
    left = live * (diag_ref[...] - sums[...])
    top_left = jnp.max(left)
    top_diag = jnp.max(live * diag_ref[...])
    spot = lax.broadcasted_iota(jnp.int32, (1, 128), 1)
    top_ref[...] = jnp.where(spot < 64, top_left, top_diag)
    for n, (start, count) in enumerate(CHUNKS):
        send(start, count, n).wait()


def panels(everybody, pivots, live_blocks, diag, chol_done, new_cols):
    vmem = pl.BlockSpec(memory_space=pltpu.VMEM)
    hbm = pl.BlockSpec(memory_space=pl.ANY)
    return pl.pallas_call(
        panel_kernel,
        out_shape=(jax.ShapeDtypeStruct((ROWS, COLS), F32), jax.ShapeDtypeStruct((1, 128), F32)),
        in_specs=[vmem, vmem, pl.BlockSpec(memory_space=pltpu.SMEM), vmem, vmem, vmem],
        out_specs=(hbm, vmem),
        scratch_shapes=[
            pltpu.VMEM((ROWS, COLS), F32),
            pltpu.VMEM((ROWS, 128), F32),
            pltpu.VMEM((COLS, K), F32),
            pltpu.VMEM((K, COLS), F32),
            pltpu.VMEM((K, 2 * COLS), BF16),
            pltpu.VMEM((2, ORDER, COLS), F32),
            pltpu.VMEM((ORDER, 256), F32),
            pltpu.VMEM((256, 256), BF16),
            pltpu.VMEM((256, 256), BF16),
            pltpu.VMEM((256, 1024), BF16),
            pltpu.VMEM((38, 128), F32),
            pltpu.SemaphoreType.DMA((len(CHUNKS),)),
        ],
        compiler_params=pltpu.CompilerParams(vmem_limit_bytes=VMEM_LIMIT),
    )(everybody, pivots, live_blocks, diag, chol_done, new_cols)


def top_kernel(in_ref, out_ref, table, own_sem, send_sem, recv_sem):
    grp, blk = lax.axis_index("grp"), lax.axis_index("blk")
    x, y = lax.div(blk, 4), lax.rem(blk, 4)
    peers = (
        [(lax.rem(grp + k, 8), blk) for k in range(1, 8)],
        [(grp, lax.rem(x + k, 4) * 4 + y) for k in range(1, 4)],
        [(grp, x * 4 + lax.rem(y + k, 4)) for k in range(1, 4)],
    )
    barrier = pltpu.get_barrier_semaphore()
    for group in peers:
        for there in group:
            pl.semaphore_signal(barrier, inc=1, device_id=there, device_id_type=MESH)
    mine = table.at[x, y, grp]
    own = pltpu.make_async_copy(in_ref, mine, own_sem)
    own.start()
    pl.semaphore_wait(barrier, 13)
    sent = []
    for phase, (source, target) in enumerate(
        ((in_ref, mine), (table.at[x, y], table.at[x, y]), (table.at[:, y], table.at[:, y]))
    ):
        if phase == 1:
            own.wait()
        flying = []
        for n, there in enumerate(peers[phase]):
            copy = pltpu.make_async_remote_copy(
                src_ref=source, dst_ref=target, send_sem=send_sem.at[phase, n], recv_sem=recv_sem.at[phase, n],
                device_id=there, device_id_type=MESH,
            )
            copy.start()
            flying.append(copy)
        for copy in flying:
            copy.wait_recv()
        sent += flying
    best = jnp.max(table[...].reshape(128, 128), axis=0, keepdims=True)
    spot = lax.broadcasted_iota(jnp.int32, (1, 128), 1)
    low = -3.0e38
    left = jnp.max(jnp.where(spot < 64, best, low), axis=1, keepdims=True)
    diag = jnp.max(jnp.where(spot < 64, low, best), axis=1, keepdims=True)
    out_ref[...] = jnp.broadcast_to(left / diag, (1, 128))
    for copy in sent:
        copy.wait_send()


def top(mine):
    return pl.pallas_call(
        top_kernel,
        out_shape=jax.ShapeDtypeStruct((1, 128), F32),
        in_specs=[pl.BlockSpec(memory_space=pltpu.VMEM)],
        out_specs=pl.BlockSpec(memory_space=pltpu.VMEM),
        scratch_shapes=[
            pltpu.VMEM((4, 4, 8, 1, 128), F32),
            pltpu.SemaphoreType.DMA,
            pltpu.SemaphoreType.DMA((3, 7)),
            pltpu.SemaphoreType.DMA((3, 7)),
        ],
        compiler_params=pltpu.CompilerParams(collective_id=1, has_side_effects=True, vmem_limit_bytes=2 * 1024 * 1024),
    )(mine)


def body(chol_done, new_cols, diag_entries, pivots, live_blocks):
    slots = pick(pivots, chol_done, new_cols)
    everybody = gather(slots).reshape(128 * SLOT_ROWS, 128)
    diag = diag_entries.reshape(ROWS // 128, 128)
    vectors, mine = panels(everybody, pivots, live_blocks, diag, chol_done, new_cols)
    return vectors, top(mine)[0, 0:1]


def solution(mesh):
    placed = (P(("grp", "blk"), None), P(("grp", "blk"), None), P(("grp", "blk")), P(), P())
    return jax.shard_map(
        body, mesh=mesh, in_specs=placed, out_specs=(P(("grp", "blk"), None), P()), check_vma=False
    )
```

```python
import jax
import jax.numpy as jnp
from jax import lax
from jax.experimental import pallas as pl
from jax.experimental.pallas import tpu as pltpu
from jax.sharding import PartitionSpec as P

MESH = pl.DeviceIdType.MESH
F32 = jnp.float32
BF16 = jnp.bfloat16
ROWS = 4864
K = 512
ORDER = 192
COLS = 384
BLOCK_ROWS = 256
SLOTS = 3
SLOT_ROWS = 40
STEP = 16
ROUNDS = ORDER // STEP
BIG = 768
TILE = 384
CHUNKS = [(i * BIG, BIG) for i in range(ROWS // BIG)] + [(ROWS // BIG * BIG, ROWS % BIG)]
VMEM_LIMIT = 24 * 1024 * 1024
COLOURS = ((0, 16, "yxz"), (16, 16, "xzy"), (32, 8, "zyx"))


def slot_base(panel, slot):
    return slot * 6 if panel == 0 else 18 + slot * 7


def pick_kernel(piv_ref, chol_hbm, cols_hbm, out_ref, cbuf, nbuf, sem):
    me = lax.axis_index("grp") * 16 + lax.axis_index("blk")
    base = me * ROWS
    local = piv_ref[...] - base
    mine = (local >= 0) & (local < ROWS)
    spot = lax.broadcasted_iota(jnp.int32, (2, ORDER), 1)
    key = jnp.where(mine, (spot * 8192 + local).astype(F32), 4.0e6)
    found = []
    for slot in range(SLOTS):
        least = jnp.min(key, axis=1, keepdims=True)
        found.append(least)
        key = jnp.where(key <= least, 4.0e6, key)
    copies = []
    where_row = []
    for panel in range(2):
        for slot in range(SLOTS):
            value = found[slot][panel, 0].astype(jnp.int32)
            row = jnp.where(value < 4000000, value & 8191, 0)
            row = jnp.minimum(row, ROWS - 1)
            group = pl.multiple_of((row // 8) * 8, 8)
            n = panel * SLOTS + slot
            one = pltpu.make_async_copy(chol_hbm.at[pl.ds(group, 8)], cbuf.at[n], sem.at[0, n])
            two = pltpu.make_async_copy(cols_hbm.at[pl.ds(group, 8)], nbuf.at[n], sem.at[1, n])
            one.start()
            two.start()
            copies.append((one, two))
            where_row.append(row - group)
    for panel in range(2):
        for slot in range(SLOTS):
            n = panel * SLOTS + slot
            for copy in copies[n]:
                copy.wait()
            at = slot_base(panel, slot)
            sub = lax.broadcasted_iota(jnp.int32, (8, 128), 0) == where_row[n]
            for c in range(6 if panel == 0 else 7):
                tile = cbuf[n, :, c * 128 : c * 128 + 128] if c < 4 else nbuf[n, :, (c - 4) * 128 : (c - 3) * 128]
                out_ref[at + c : at + c + 1, :] = jnp.sum(jnp.where(sub, tile, 0.0), axis=0, keepdims=True)
    out_ref[39:40, :] = jnp.zeros((1, 128), F32)


def pick(pivots, chol_done, new_cols):
    return pl.pallas_call(
        pick_kernel,
        out_shape=jax.ShapeDtypeStruct((SLOT_ROWS, 128), F32),
        in_specs=[
            pl.BlockSpec(memory_space=pltpu.VMEM),
            pl.BlockSpec(memory_space=pltpu.HBM),
            pl.BlockSpec(memory_space=pltpu.HBM),
        ],
        out_specs=pl.BlockSpec(memory_space=pltpu.VMEM),
        scratch_shapes=[
            pltpu.VMEM((6, 8, K), F32),
            pltpu.VMEM((6, 8, COLS), F32),
            pltpu.SemaphoreType.DMA((2, 6)),
        ],
        compiler_params=pltpu.CompilerParams(vmem_limit_bytes=50 * 1024 * 1024),
    )(pivots, chol_done, new_cols)


def gather_kernel(in_ref, g_ref, own_sem, send_sem, recv_sem, pass_send, pass_recv):
    grp, blk = lax.axis_index("grp"), lax.axis_index("blk")
    at = {"z": lax.div(grp, 2), "x": lax.div(blk, 4), "y": lax.rem(blk, 4)}
    core = lax.rem(grp, 2)

    def device(z, c, x, y):
        return (z * 2 + c, x * 4 + y)

    def beside(axis, k):
        there = dict(at)
        there[axis] = lax.rem(at[axis] + k, 4)
        return device(there["z"], core, there["x"], there["y"])

    partner = device(at["z"], 1 - core, at["x"], at["y"])
    barrier = pltpu.get_barrier_semaphore()
    for axis in "xyz":
        for k in (1, 2, 3):
            pl.semaphore_signal(barrier, inc=1, device_id=beside(axis, k), device_id_type=MESH)
    pl.semaphore_signal(barrier, inc=1, device_id=partner, device_id_type=MESH)
    own = pltpu.make_async_copy(in_ref, g_ref.at[at["z"], core, at["x"], at["y"]], own_sem)
    own.start()
    pl.semaphore_wait(barrier, 10)

    def region(colour, have, fixed):
        first, count, _ = COLOURS[colour]
        pick_at = [slice(None) if a in have else fixed[a] for a in "zxy"]
        return g_ref.at[pick_at[0], core, pick_at[1], pick_at[2], pl.ds(first, count), :]

    flights = {}

    def launch(colour, phase):
        first, count, order = COLOURS[colour]
        have = order[:phase]
        here = region(colour, have, at)
        for k in (2, 1, 3):
            source = in_ref.at[pl.ds(first, count), :] if phase == 0 else here
            copy = pltpu.make_async_remote_copy(
                src_ref=source,
                dst_ref=here,
                send_sem=send_sem.at[colour, phase, k - 1],
                recv_sem=recv_sem.at[colour, phase, k - 1],
                device_id=beside(order[phase], k),
                device_id_type=MESH,
            )
            copy.start()
            flights[colour, phase, k] = copy

    passes = []

    def hand_over(colour, piece, ref):
        copy = pltpu.make_async_remote_copy(
            src_ref=ref,
            dst_ref=ref,
            send_sem=pass_send.at[colour, piece],
            recv_sem=pass_recv.at[colour, piece],
            device_id=partner,
            device_id_type=MESH,
        )
        copy.start()
        passes.append(copy)

    colours = range(len(COLOURS))
    for colour in colours:
        launch(colour, 0)
    own.wait()
    for phase in (1, 2):
        for colour in colours:
            for k in (1, 3, 2):
                flights[colour, phase - 1, k].wait_recv()
            launch(colour, phase)
            if phase == 2:
                hand_over(colour, 0, region(colour, COLOURS[colour][2][:2], at))
    for k in (1, 3, 2):
        for colour in colours:
            flights[colour, 2, k].wait_recv()
            last = COLOURS[colour][2][2]
            there = dict(at)
            there[last] = lax.rem(at[last] + (4 - k), 4)
            hand_over(colour, k, region(colour, COLOURS[colour][2][:2], there))
    for copy in passes:
        copy.wait_recv()
    for copy in passes:
        copy.wait_send()
    for copy in flights.values():
        copy.wait_send()


def gather(slots):
    return pl.pallas_call(
        gather_kernel,
        out_shape=jax.ShapeDtypeStruct((4, 2, 4, 4, SLOT_ROWS, 128), F32),
        in_specs=[pl.BlockSpec(memory_space=pltpu.VMEM)],
        out_specs=pl.BlockSpec(memory_space=pltpu.VMEM),
        scratch_shapes=[
            pltpu.SemaphoreType.DMA,
            pltpu.SemaphoreType.DMA((3, 3, 3)),
            pltpu.SemaphoreType.DMA((3, 3, 3)),
            pltpu.SemaphoreType.DMA((3, 4)),
            pltpu.SemaphoreType.DMA((3, 4)),
        ],
        compiler_params=pltpu.CompilerParams(collective_id=0, has_side_effects=True, vmem_limit_bytes=4 * 1024 * 1024),
        cost_estimate=pl.CostEstimate(flops=20_000_000_000, bytes_accessed=2_700_000, transcendentals=0),
    )(slots)


def split2(a):
    high = a.astype(BF16)
    return high, (a - high.astype(F32)).astype(BF16)


def split3(a):
    high = a.astype(BF16)
    rest = a - high.astype(F32)
    mid = rest.astype(BF16)
    return high, mid, (rest - mid.astype(F32)).astype(BF16)


def mul(a, b):
    return jnp.dot(a, b, preferred_element_type=F32)


def mul3(a, b_high, b_low):
    high, low = split2(a)
    return mul(high, b_high) + (mul(high, b_low) + mul(low, b_high))


def over_lanes(x, lane):
    return jnp.take_along_axis(x, jnp.full((8, 128), lane, jnp.int32), axis=1)


def over_rows(x, row):
    return jnp.broadcast_to(x[row : row + 1, :], (8, 128))


def factor_round(a_ref, r, off):
    rs = pl.multiple_of(r * STEP, STEP)
    c0 = off + r * STEP
    t = c0 // 128
    l0 = c0 - t * 128
    tl = pl.multiple_of(t * 128, 128)
    lane = lax.broadcasted_iota(jnp.int32, (8, 128), 1)
    sub = lax.broadcasted_iota(jnp.int32, (8, 128), 0)
    raw = [a_ref[pl.ds(rs + 8 * q, 8), pl.ds(tl, 128)] for q in range(2)]
    col = {}
    for j in range(STEP):
        for q in range(j // 8, 2):
            col[j, q] = over_lanes(raw[q], l0 + j)
    row = {}
    for q in range(2):
        for h in range(2):
            x = a_ref[pl.ds(rs + 8 * q, 8), h * 128 : (h + 1) * 128]
            rel = lane + (h * 128) - c0
            unit = jnp.where(rel == sub + 8 * q, 1.0, 0.0)
            row[q, h] = jnp.where((rel >= 0) & (rel < STEP), unit, x)
    for j in range(STEP):
        jq, js = j // 8, j % 8
        scale = lax.rsqrt(over_rows(col[j, jq], js))
        low = {q: col[j, q] * scale for q in range(jq, 2)}
        for m in range(j + 1, STEP):
            times = over_rows(low[m // 8], m % 8)
            for q in range(m // 8, 2):
                col[m, q] = col[m, q] - low[q] * times
        low[jq] = jnp.where(sub > js, low[jq], 0.0)
        for h in range(2):
            lead = over_rows(row[jq, h], js) * scale
            for q in range(jq, 2):
                row[q, h] = row[q, h] - low[q] * lead
            row[jq, h] = jnp.where(sub == js, lead, row[jq, h])
    for q in range(2):
        for h in range(2):
            a_ref[pl.ds(rs + 8 * q, 8), h * 128 : (h + 1) * 128] = row[q, h]
    u = jnp.concatenate([jnp.concatenate([row[q, h] for h in range(2)], axis=1) for q in range(2)], axis=0)
    lanes = lax.broadcasted_iota(jnp.int32, (STEP, 256), 1)
    high, mid, low3 = split3(u)
    zero = jnp.zeros_like(u)
    ahead = lanes >= c0 + STEP
    h_l, m_l, l_l = split3(jnp.where(ahead, u, zero))
    left = jnp.concatenate([h_l, h_l, m_l, m_l, h_l, l_l], axis=0)
    right = jnp.concatenate([high, mid, high, mid, low3, high], axis=0)
    z = lax.dot_general(left, right, (((0,), (0,)), ((), ())), preferred_element_type=F32)
    rows_i = lax.broadcasted_iota(jnp.int32, (ORDER, 256), 0)
    cols_i = lax.broadcasted_iota(jnp.int32, (ORDER, 256), 1)
    old = (rows_i >= rs + STEP) & (cols_i >= c0) & (cols_i < c0 + STEP)
    a_ref[...] = jnp.where(old, 0.0, a_ref[...]) - z[off : off + ORDER, :]


def lower_only(a, off):
    row = lax.broadcasted_iota(jnp.int32, (ORDER, 256), 0)
    col = lax.broadcasted_iota(jnp.int32, (ORDER, 256), 1) - off
    return jnp.where((col >= 0) & (col <= row), a, 0.0)


def panel_kernel(g_ref, piv_ref, live_ref, diag_ref, chol, cols, out_hbm, top_ref,
                 rbuf, squares, hmat, ht_pair, head, a_ref,
                 v_high, v_low, w_pair, sums, out_sem):
    me = lax.axis_index("grp") * 16 + lax.axis_index("blk")
    alive = live_ref[me] * BLOCK_ROWS

    q_i = lax.broadcasted_iota(jnp.int32, (ORDER, ORDER), 1)
    p_i = lax.broadcasted_iota(jnp.int32, (ORDER, ORDER), 0)
    for panel in range(2):
        owner_row = (piv_ref[panel : panel + 1, :] // ROWS).astype(F32)
        owner_all = jnp.broadcast_to(owner_row, (ORDER, ORDER))
        owner = jnp.sum(jnp.where(q_i == p_i, owner_all, 0.0), axis=1, keepdims=True)
        before = (owner_all == owner) & (q_i < p_i)
        rank = jnp.sum(jnp.where(before, 1.0, 0.0), axis=1, keepdims=True)
        dev = lax.broadcasted_iota(jnp.int32, (ORDER, 128), 1).astype(F32)
        hot = jnp.concatenate(
            [jnp.where((dev == owner) & (rank == float(s)), 1.0, 0.0) for s in range(SLOTS)], axis=1
        ).astype(BF16)
        def chunk(c):
            pieces = [g_ref[pl.ds(slot_base(panel, s) + c, 128, stride=SLOT_ROWS), :] for s in range(SLOTS)]
            return jnp.concatenate(pieces, axis=0)

        mine = pl.ds(panel * ORDER, ORDER)
        for c in (0, 2):
            high, low = split2(jnp.concatenate([chunk(c), chunk(c + 1)], axis=1))
            hmat[mine, c * 128 : (c + 2) * 128] = mul(hot, high) + mul(hot, low)
        high, mid, low = split3(jnp.concatenate([chunk(4), chunk(5)], axis=1))
        head[panel, :, 0:256] = mul(hot, high) + (mul(hot, mid) + mul(hot, low))
        if panel == 1:
            high, mid, low = split3(chunk(6))
            head[panel, :, 256:384] = mul(hot, high) + (mul(hot, mid) + mul(hot, low))
    high, low = split2(hmat[...].T)
    ht_pair[:, 0:COLS] = high
    ht_pair[:, COLS:] = low

    lanes = lax.broadcasted_iota(jnp.int32, (ORDER, 256), 1)
    known = mul3(hmat[...], ht_pair[:, 0:COLS], ht_pair[:, COLS:])
    a_ref[...] = jnp.where(lanes < ORDER, head[0, :, 0:256] - known[0:ORDER, 0:256], 0.0)
    head[1, :, :] = head[1, :, :] - known[ORDER:, :]

    def residual_high(start, count):
        rows = pl.ds(start, count)
        both = mul(chol[rows, :].astype(BF16), ht_pair[...])
        rbuf[rows, :] = cols[rows, :] - (both[:, 0:COLS] + both[:, COLS:])

    def residual_low(start, count):
        rows = pl.ds(start, count)
        tile = chol[rows, :]
        left = rbuf[rows, :] - mul(split2(tile)[1], ht_pair[:, 0:COLS])
        spot = lax.broadcasted_iota(jnp.int32, (count, COLS), 0) + start
        rbuf[rows, :] = jnp.where(spot < alive, left, 0.0)
        square = tile * tile
        squares[rows, :] = (square[:, 0:128] + square[:, 128:256]) + (square[:, 256:384] + square[:, 384:512])

    def round_one(r, _):
        start = pl.multiple_of(r * BIG, BIG)
        residual_high(start, BIG)
        factor_round(a_ref, 2 * r, 0)
        residual_low(start, BIG)
        factor_round(a_ref, 2 * r + 1, 0)
        return 0

    lax.fori_loop(0, ROUNDS // 2, round_one, 0)
    residual_high(*CHUNKS[-1])
    residual_low(*CHUNKS[-1])

    pad = jnp.zeros((64, 256), F32)
    v_one = jnp.concatenate([lower_only(a_ref[...], 0), pad], axis=0).T
    high, low = split2(v_one)
    w_pair[:, 0:256] = high
    w_pair[:, 512:768] = low
    f_rows = mul3(head[1, :, 0:256], high, low)
    f_tr = jnp.concatenate([pad, f_rows], axis=0).T
    high, low = split2(f_tr)
    two = head[1, :, 128:384] - mul3(f_rows, high, low)
    a_ref[...] = jnp.where(lanes >= 64, two, 0.0)
    high, low = split2(mul3(v_one, high, low))
    w_pair[:, 256:512] = high
    w_pair[:, 768:] = low

    def first_of(start, count):
        rows = pl.ds(start, count)
        high, low = split2(rbuf[rows, 0:256])
        wide = mul(high, w_pair[...])
        both = (wide[:, 0:512] + wide[:, 512:]) + mul(low, w_pair[:, 0:512])
        first = both[:, 0:256]
        rest = rbuf[rows, 128:384] - both[:, 256:512]
        rbuf[rows, 0:128] = first[:, 0:128]
        spot = lax.broadcasted_iota(jnp.int32, (count, 128), 1)
        rbuf[rows, 128:256] = jnp.where(spot < 64, first[:, 128:256], rest[:, 0:128])
        rbuf[rows, 256:384] = rest[:, 128:256]
        squares[rows, :] = squares[rows, :] + (first[:, 0:128] * first[:, 0:128] + first[:, 128:256] * first[:, 128:256])

    def round_two(r, _):
        first_of(pl.multiple_of(r * TILE, TILE), TILE)
        factor_round(a_ref, r, 64)
        return 0

    lax.fori_loop(0, ROUNDS, round_two, 0)
    first_of(*CHUNKS[-1])

    v_two = jnp.concatenate([pad, lower_only(a_ref[...], 64)], axis=0).T
    high, low = split2(v_two)
    v_high[...] = high
    v_low[...] = low

    def send(start, count, n):
        rows = pl.ds(start, count)
        return pltpu.make_async_copy(rbuf.at[rows], out_hbm.at[rows], out_sem.at[n])

    def second_of(start, count, n, at):
        rows = pl.ds(start, count)
        second = mul3(rbuf[rows, 128:384], v_high[...], v_low[...])
        spot = lax.broadcasted_iota(jnp.int32, (count, 128), 1)
        rbuf[rows, 128:256] = jnp.where(spot < 64, rbuf[rows, 128:256], second[:, 0:128])
        rbuf[rows, 256:384] = second[:, 128:256]
        send(start, count, n).start()
        square = squares[rows, :] + (second[:, 0:128] * second[:, 0:128] + second[:, 128:256] * second[:, 128:256])
        for q in range(count // 128):
            turned = square[q * 128 : (q + 1) * 128, :].T
            sums[pl.ds(at + q, 1), :] = jnp.sum(turned, axis=0, keepdims=True)

    def round_three(r, _):
        second_of(pl.multiple_of(r * BIG, BIG), BIG, r, r * (BIG // 128))
        return 0

    lax.fori_loop(0, ROWS // BIG, round_three, 0)
    second_of(*CHUNKS[-1], len(CHUNKS) - 1, CHUNKS[-1][0] // 128)

    entry = lax.broadcasted_iota(jnp.int32, (38, 128), 0) * 128 + lax.broadcasted_iota(jnp.int32, (38, 128), 1)
    live = jnp.where(entry < alive, 1.0, 0.0)
    left = live * (diag_ref[...] - sums[...])
    top_left = jnp.max(left)
    top_diag = jnp.max(live * diag_ref[...])
    spot = lax.broadcasted_iota(jnp.int32, (1, 128), 1)
    top_ref[...] = jnp.where(spot < 64, top_left, top_diag)
    for n, (start, count) in enumerate(CHUNKS):
        send(start, count, n).wait()


def panels(everybody, pivots, live_blocks, diag, chol_done, new_cols):
    vmem = pl.BlockSpec(memory_space=pltpu.VMEM)
    hbm = pl.BlockSpec(memory_space=pl.ANY)
    return pl.pallas_call(
        panel_kernel,
        out_shape=(jax.ShapeDtypeStruct((ROWS, COLS), F32), jax.ShapeDtypeStruct((1, 128), F32)),
        in_specs=[vmem, vmem, pl.BlockSpec(memory_space=pltpu.SMEM), vmem, vmem, vmem],
        out_specs=(hbm, vmem),
        scratch_shapes=[
            pltpu.VMEM((ROWS, COLS), F32),
            pltpu.VMEM((ROWS, 128), F32),
            pltpu.VMEM((COLS, K), F32),
            pltpu.VMEM((K, 2 * COLS), BF16),
            pltpu.VMEM((2, ORDER, COLS), F32),
            pltpu.VMEM((ORDER, 256), F32),
            pltpu.VMEM((256, 256), BF16),
            pltpu.VMEM((256, 256), BF16),
            pltpu.VMEM((256, 1024), BF16),
            pltpu.VMEM((38, 128), F32),
            pltpu.SemaphoreType.DMA((len(CHUNKS),)),
        ],
        compiler_params=pltpu.CompilerParams(vmem_limit_bytes=VMEM_LIMIT),
    )(everybody, pivots, live_blocks, diag, chol_done, new_cols)


def top_kernel(in_ref, out_ref, table, own_sem, send_sem, recv_sem):
    grp, blk = lax.axis_index("grp"), lax.axis_index("blk")
    x, y = lax.div(blk, 4), lax.rem(blk, 4)
    peers = (
        [(lax.rem(grp + k, 8), blk) for k in range(1, 8)],
        [(grp, lax.rem(x + k, 4) * 4 + y) for k in range(1, 4)],
        [(grp, x * 4 + lax.rem(y + k, 4)) for k in range(1, 4)],
    )
    barrier = pltpu.get_barrier_semaphore()
    for group in peers:
        for there in group:
            pl.semaphore_signal(barrier, inc=1, device_id=there, device_id_type=MESH)
    mine = table.at[x, y, grp]
    own = pltpu.make_async_copy(in_ref, mine, own_sem)
    own.start()
    pl.semaphore_wait(barrier, 13)
    sent = []
    for phase, (source, target) in enumerate(
        ((in_ref, mine), (table.at[x, y], table.at[x, y]), (table.at[:, y], table.at[:, y]))
    ):
        if phase == 1:
            own.wait()
        flying = []
        for n, there in enumerate(peers[phase]):
            copy = pltpu.make_async_remote_copy(
                src_ref=source, dst_ref=target, send_sem=send_sem.at[phase, n], recv_sem=recv_sem.at[phase, n],
                device_id=there, device_id_type=MESH,
            )
            copy.start()
            flying.append(copy)
        for copy in flying:
            copy.wait_recv()
        sent += flying
    best = jnp.max(table[...].reshape(128, 128), axis=0, keepdims=True)
    spot = lax.broadcasted_iota(jnp.int32, (1, 128), 1)
    low = -3.0e38
    left = jnp.max(jnp.where(spot < 64, best, low), axis=1, keepdims=True)
    diag = jnp.max(jnp.where(spot < 64, low, best), axis=1, keepdims=True)
    out_ref[...] = jnp.broadcast_to(left / diag, (1, 128))
    for copy in sent:
        copy.wait_send()


def top(mine):
    return pl.pallas_call(
        top_kernel,
        out_shape=jax.ShapeDtypeStruct((1, 128), F32),
        in_specs=[pl.BlockSpec(memory_space=pltpu.VMEM)],
        out_specs=pl.BlockSpec(memory_space=pltpu.VMEM),
        scratch_shapes=[
            pltpu.VMEM((4, 4, 8, 1, 128), F32),
            pltpu.SemaphoreType.DMA,
            pltpu.SemaphoreType.DMA((3, 7)),
            pltpu.SemaphoreType.DMA((3, 7)),
        ],
        compiler_params=pltpu.CompilerParams(collective_id=1, has_side_effects=True, vmem_limit_bytes=2 * 1024 * 1024),
    )(mine)


def body(chol_done, new_cols, diag_entries, pivots, live_blocks):
    slots = pick(pivots, chol_done, new_cols)
    everybody = gather(slots).reshape(128 * SLOT_ROWS, 128)
    diag = diag_entries.reshape(ROWS // 128, 128)
    vectors, mine = panels(everybody, pivots, live_blocks, diag, chol_done, new_cols)
    return vectors, top(mine)[0, 0:1]


def solution(mesh):
    placed = (P(("grp", "blk"), None), P(("grp", "blk"), None), P(("grp", "blk")), P(), P())
    return jax.shard_map(
        body, mesh=mesh, in_specs=placed, out_specs=(P(("grp", "blk"), None), P()), check_vma=False
    )
```

```python
import jax
import jax.numpy as jnp
from jax import lax
from jax.experimental import pallas as pl
from jax.experimental.pallas import tpu as pltpu
from jax.sharding import PartitionSpec as P

MESH = pl.DeviceIdType.MESH
F32 = jnp.float32
BF16 = jnp.bfloat16
ROWS = 4864
K = 512
ORDER = 192
COLS = 384
BLOCK_ROWS = 256
SLOTS = 3
SLOT_ROWS = 40
STEP = 16
ROUNDS = ORDER // STEP
BIG = 768
TILE = 384
CHUNKS = [(i * BIG, BIG) for i in range(ROWS // BIG)] + [(ROWS // BIG * BIG, ROWS % BIG)]
VMEM_LIMIT = 24 * 1024 * 1024
COLOURS = ((0, 13, "yxz"), (13, 13, "xzy"), (26, 13, "zyx"))


def slot_base(panel, slot):
    return slot * 6 if panel == 0 else 18 + slot * 7


def pick_kernel(piv_ref, chol_hbm, cols_hbm, out_ref, cbuf, nbuf, sem):
    me = lax.axis_index("grp") * 16 + lax.axis_index("blk")
    base = me * ROWS
    local = piv_ref[...] - base
    mine = (local >= 0) & (local < ROWS)
    spot = lax.broadcasted_iota(jnp.int32, (2, ORDER), 1)
    key = jnp.where(mine, (spot * 8192 + local).astype(F32), 4.0e6)
    found = []
    for slot in range(SLOTS):
        least = jnp.min(key, axis=1, keepdims=True)
        found.append(least)
        key = jnp.where(key <= least, 4.0e6, key)
    copies = []
    where_row = []
    for panel in range(2):
        for slot in range(SLOTS):
            value = found[slot][panel, 0].astype(jnp.int32)
            row = jnp.where(value < 4000000, value & 8191, 0)
            row = jnp.minimum(row, ROWS - 1)
            group = pl.multiple_of((row // 8) * 8, 8)
            n = panel * SLOTS + slot
            one = pltpu.make_async_copy(chol_hbm.at[pl.ds(group, 8)], cbuf.at[n], sem.at[0, n])
            two = pltpu.make_async_copy(cols_hbm.at[pl.ds(group, 8)], nbuf.at[n], sem.at[1, n])
            one.start()
            two.start()
            copies.append((one, two))
            where_row.append(row - group)
    for panel in range(2):
        for slot in range(SLOTS):
            n = panel * SLOTS + slot
            for copy in copies[n]:
                copy.wait()
            at = slot_base(panel, slot)
            sub = lax.broadcasted_iota(jnp.int32, (8, 128), 0) == where_row[n]
            for c in range(6 if panel == 0 else 7):
                tile = cbuf[n, :, c * 128 : c * 128 + 128] if c < 4 else nbuf[n, :, (c - 4) * 128 : (c - 3) * 128]
                out_ref[at + c : at + c + 1, :] = jnp.sum(jnp.where(sub, tile, 0.0), axis=0, keepdims=True)
    out_ref[39:40, :] = jnp.zeros((1, 128), F32)


def pick(pivots, chol_done, new_cols):
    return pl.pallas_call(
        pick_kernel,
        out_shape=jax.ShapeDtypeStruct((SLOT_ROWS, 128), F32),
        in_specs=[
            pl.BlockSpec(memory_space=pltpu.VMEM),
            pl.BlockSpec(memory_space=pltpu.HBM),
            pl.BlockSpec(memory_space=pltpu.HBM),
        ],
        out_specs=pl.BlockSpec(memory_space=pltpu.VMEM),
        scratch_shapes=[
            pltpu.VMEM((6, 8, K), F32),
            pltpu.VMEM((6, 8, COLS), F32),
            pltpu.SemaphoreType.DMA((2, 6)),
        ],
        compiler_params=pltpu.CompilerParams(vmem_limit_bytes=50 * 1024 * 1024),
    )(pivots, chol_done, new_cols)


def gather_kernel(in_ref, g_ref, own_sem, send_sem, recv_sem, pass_send, pass_recv):
    grp, blk = lax.axis_index("grp"), lax.axis_index("blk")
    at = {"z": lax.div(grp, 2), "x": lax.div(blk, 4), "y": lax.rem(blk, 4)}
    core = lax.rem(grp, 2)

    def device(z, c, x, y):
        return (z * 2 + c, x * 4 + y)

    def beside(axis, k):
        there = dict(at)
        there[axis] = lax.rem(at[axis] + k, 4)
        return device(there["z"], core, there["x"], there["y"])

    partner = device(at["z"], 1 - core, at["x"], at["y"])
    barrier = pltpu.get_barrier_semaphore()
    for axis in "xyz":
        for k in (1, 2, 3):
            pl.semaphore_signal(barrier, inc=1, device_id=beside(axis, k), device_id_type=MESH)
    pl.semaphore_signal(barrier, inc=1, device_id=partner, device_id_type=MESH)
    own = pltpu.make_async_copy(in_ref, g_ref.at[at["z"], core, at["x"], at["y"]], own_sem)
    own.start()
    pl.semaphore_wait(barrier, 10)

    def region(colour, have, fixed):
        first, count, _ = COLOURS[colour]
        pick_at = [slice(None) if a in have else fixed[a] for a in "zxy"]
        return g_ref.at[pick_at[0], core, pick_at[1], pick_at[2], pl.ds(first, count), :]

    flights = {}

    def launch(colour, phase):
        first, count, order = COLOURS[colour]
        have = order[:phase]
        here = region(colour, have, at)
        for k in (2, 1, 3):
            source = in_ref.at[pl.ds(first, count), :] if phase == 0 else here
            copy = pltpu.make_async_remote_copy(
                src_ref=source,
                dst_ref=here,
                send_sem=send_sem.at[colour, phase, k - 1],
                recv_sem=recv_sem.at[colour, phase, k - 1],
                device_id=beside(order[phase], k),
                device_id_type=MESH,
            )
            copy.start()
            flights[colour, phase, k] = copy

    passes = []

    def hand_over(colour, piece, ref):
        copy = pltpu.make_async_remote_copy(
            src_ref=ref,
            dst_ref=ref,
            send_sem=pass_send.at[colour, piece],
            recv_sem=pass_recv.at[colour, piece],
            device_id=partner,
            device_id_type=MESH,
        )
        copy.start()
        passes.append(copy)

    colours = range(len(COLOURS))
    for colour in colours:
        launch(colour, 0)
    own.wait()
    for phase in (1, 2):
        for colour in colours:
            for k in (1, 3, 2):
                flights[colour, phase - 1, k].wait_recv()
            launch(colour, phase)
            if phase == 2:
                hand_over(colour, 0, region(colour, COLOURS[colour][2][:2], at))
    for k in (1, 3, 2):
        for colour in colours:
            flights[colour, 2, k].wait_recv()
            last = COLOURS[colour][2][2]
            there = dict(at)
            there[last] = lax.rem(at[last] + (4 - k), 4)
            hand_over(colour, k, region(colour, COLOURS[colour][2][:2], there))
    for copy in passes:
        copy.wait_recv()
    for copy in passes:
        copy.wait_send()
    for copy in flights.values():
        copy.wait_send()


def gather(slots):
    return pl.pallas_call(
        gather_kernel,
        out_shape=jax.ShapeDtypeStruct((4, 2, 4, 4, SLOT_ROWS, 128), F32),
        in_specs=[pl.BlockSpec(memory_space=pltpu.VMEM)],
        out_specs=pl.BlockSpec(memory_space=pltpu.VMEM),
        scratch_shapes=[
            pltpu.SemaphoreType.DMA,
            pltpu.SemaphoreType.DMA((3, 3, 3)),
            pltpu.SemaphoreType.DMA((3, 3, 3)),
            pltpu.SemaphoreType.DMA((3, 4)),
            pltpu.SemaphoreType.DMA((3, 4)),
        ],
        compiler_params=pltpu.CompilerParams(collective_id=0, has_side_effects=True, vmem_limit_bytes=4 * 1024 * 1024),
        cost_estimate=pl.CostEstimate(flops=20_000_000_000, bytes_accessed=2_700_000, transcendentals=0),
    )(slots)


def split2(a):
    high = a.astype(BF16)
    return high, (a - high.astype(F32)).astype(BF16)


def split3(a):
    high = a.astype(BF16)
    rest = a - high.astype(F32)
    mid = rest.astype(BF16)
    return high, mid, (rest - mid.astype(F32)).astype(BF16)


def mul(a, b):
    return jnp.dot(a, b, preferred_element_type=F32)


def mul3(a, b_high, b_low):
    high, low = split2(a)
    return mul(high, b_high) + (mul(high, b_low) + mul(low, b_high))


def over_lanes(x, lane):
    return jnp.take_along_axis(x, jnp.full((8, 128), lane, jnp.int32), axis=1)


def over_rows(x, row):
    return jnp.broadcast_to(x[row : row + 1, :], (8, 128))


def factor_round(a_ref, left_ref, right_ref, r, off):
    rs = pl.multiple_of(r * STEP, STEP)
    c0 = off + r * STEP
    t = c0 // 128
    l0 = c0 - t * 128
    tl = pl.multiple_of(t * 128, 128)
    lane = lax.broadcasted_iota(jnp.int32, (8, 128), 1)
    sub = lax.broadcasted_iota(jnp.int32, (8, 128), 0)
    raw = [a_ref[pl.ds(rs + 8 * q, 8), pl.ds(tl, 128)] for q in range(2)]
    col = {}
    for j in range(STEP):
        for q in range(j // 8, 2):
            col[j, q] = over_lanes(raw[q], l0 + j)
    row = {}
    for q in range(2):
        for h in range(2):
            x = a_ref[pl.ds(rs + 8 * q, 8), h * 128 : (h + 1) * 128]
            rel = lane + (h * 128) - c0
            unit = jnp.where(rel == sub + 8 * q, 1.0, 0.0)
            row[q, h] = jnp.where((rel >= 0) & (rel < STEP), unit, x)
    for j in range(STEP):
        jq, js = j // 8, j % 8
        scale = lax.rsqrt(over_rows(col[j, jq], js))
        low = {q: col[j, q] * scale for q in range(jq, 2)}
        for m in range(j + 1, STEP):
            times = over_rows(low[m // 8], m % 8)
            for q in range(m // 8, 2):
                col[m, q] = col[m, q] - low[q] * times
        low[jq] = jnp.where(sub > js, low[jq], 0.0)
        for h in range(2):
            lead = over_rows(row[jq, h], js) * scale
            for q in range(jq, 2):
                row[q, h] = row[q, h] - low[q] * lead
            row[jq, h] = jnp.where(sub == js, lead, row[jq, h])
    for q in range(2):
        for h in range(2):
            a_ref[pl.ds(rs + 8 * q, 8), h * 128 : (h + 1) * 128] = row[q, h]
    u = jnp.concatenate([jnp.concatenate([row[q, h] for h in range(2)], axis=1) for q in range(2)], axis=0)
    lanes = lax.broadcasted_iota(jnp.int32, (STEP, 256), 1)
    high, mid, low3 = split3(u)
    h_l, m_l, l_l = split3(jnp.where(lanes >= c0 + STEP, u, 0.0))
    left_ref[...] = jnp.concatenate([h_l, h_l, m_l, m_l, h_l, l_l], axis=0)
    right_ref[...] = jnp.concatenate([high, mid, high, mid, low3, high], axis=0)


def factor_update(a_ref, left_ref, right_ref, r, off):
    c0 = off + r * STEP
    z = lax.dot_general(left_ref[...], right_ref[...], (((0,), (0,)), ((), ())), preferred_element_type=F32)
    rows_i = lax.broadcasted_iota(jnp.int32, (ORDER, 256), 0)
    cols_i = lax.broadcasted_iota(jnp.int32, (ORDER, 256), 1)
    old = (rows_i >= (r + 1) * STEP) & (cols_i >= c0) & (cols_i < c0 + STEP)
    a_ref[...] = jnp.where(old, 0.0, a_ref[...]) - z[off : off + ORDER, :]


def lower_only(a, off):
    row = lax.broadcasted_iota(jnp.int32, (ORDER, 256), 0)
    col = lax.broadcasted_iota(jnp.int32, (ORDER, 256), 1) - off
    return jnp.where((col >= 0) & (col <= row), a, 0.0)


def panel_kernel(g_ref, piv_ref, live_ref, diag_ref, chol, cols, out_hbm, top_ref,
                 rbuf, squares, hmat, ht_pair, head, a_ref, left_ref, right_ref,
                 v_high, v_low, w_pair, sums, out_sem):
    me = lax.axis_index("grp") * 16 + lax.axis_index("blk")
    alive = live_ref[me] * BLOCK_ROWS

    q_i = lax.broadcasted_iota(jnp.int32, (ORDER, ORDER), 1)
    p_i = lax.broadcasted_iota(jnp.int32, (ORDER, ORDER), 0)
    for panel in range(2):
        owner_row = (piv_ref[panel : panel + 1, :] // ROWS).astype(F32)
        owner_all = jnp.broadcast_to(owner_row, (ORDER, ORDER))
        owner = jnp.sum(jnp.where(q_i == p_i, owner_all, 0.0), axis=1, keepdims=True)
        before = (owner_all == owner) & (q_i < p_i)
        rank = jnp.sum(jnp.where(before, 1.0, 0.0), axis=1, keepdims=True)
        dev = lax.broadcasted_iota(jnp.int32, (ORDER, 128), 1).astype(F32)
        hot = jnp.concatenate(
            [jnp.where((dev == owner) & (rank == float(s)), 1.0, 0.0) for s in range(SLOTS)], axis=1
        ).astype(BF16)
        def chunk(c):
            pieces = [g_ref[pl.ds(slot_base(panel, s) + c, 128, stride=SLOT_ROWS), :] for s in range(SLOTS)]
            return jnp.concatenate(pieces, axis=0)

        mine = pl.ds(panel * ORDER, ORDER)
        for c in (0, 2):
            high, low = split2(jnp.concatenate([chunk(c), chunk(c + 1)], axis=1))
            hmat[mine, c * 128 : (c + 2) * 128] = mul(hot, high) + mul(hot, low)
        high, mid, low = split3(jnp.concatenate([chunk(4), chunk(5)], axis=1))
        head[panel, :, 0:256] = mul(hot, high) + (mul(hot, mid) + mul(hot, low))
        if panel == 1:
            high, mid, low = split3(chunk(6))
            head[panel, :, 256:384] = mul(hot, high) + (mul(hot, mid) + mul(hot, low))
    high, low = split2(hmat[...].T)
    ht_pair[:, 0:COLS] = high
    ht_pair[:, COLS:] = low

    lanes = lax.broadcasted_iota(jnp.int32, (ORDER, 256), 1)
    known = mul3(hmat[...], ht_pair[:, 0:COLS], ht_pair[:, COLS:])
    a_ref[...] = jnp.where(lanes < ORDER, head[0, :, 0:256] - known[0:ORDER, 0:256], 0.0)
    head[1, :, :] = head[1, :, :] - known[ORDER:, :]

    def residual_high(start, count):
        rows = pl.ds(start, count)
        both = mul(chol[rows, :].astype(BF16), ht_pair[...])
        rbuf[rows, :] = cols[rows, :] - (both[:, 0:COLS] + both[:, COLS:])

    def residual_low(start, count):
        rows = pl.ds(start, count)
        tile = chol[rows, :]
        left = rbuf[rows, :] - mul(split2(tile)[1], ht_pair[:, 0:COLS])
        spot = lax.broadcasted_iota(jnp.int32, (count, COLS), 0) + start
        rbuf[rows, :] = jnp.where(spot < alive, left, 0.0)
        square = tile * tile
        squares[rows, :] = (square[:, 0:128] + square[:, 128:256]) + (square[:, 256:384] + square[:, 384:512])

    def round_one(r, _):
        start = pl.multiple_of(r * BIG, BIG)
        factor_update(a_ref, left_ref, right_ref, 2 * r - 1, 0)
        residual_high(start, BIG)
        factor_round(a_ref, left_ref, right_ref, 2 * r, 0)
        factor_update(a_ref, left_ref, right_ref, 2 * r, 0)
        residual_low(start, BIG)
        factor_round(a_ref, left_ref, right_ref, 2 * r + 1, 0)
        return 0

    nothing = jnp.zeros((6 * STEP, 256), BF16)
    left_ref[...] = nothing
    right_ref[...] = nothing
    lax.fori_loop(0, ROUNDS // 2, round_one, 0)
    residual_high(*CHUNKS[-1])
    residual_low(*CHUNKS[-1])

    pad = jnp.zeros((64, 256), F32)
    v_one = jnp.concatenate([lower_only(a_ref[...], 0), pad], axis=0).T
    high, low = split2(v_one)
    w_pair[:, 0:256] = high
    w_pair[:, 512:768] = low
    f_rows = mul3(head[1, :, 0:256], high, low)
    f_tr = jnp.concatenate([pad, f_rows], axis=0).T
    high, low = split2(f_tr)
    two = head[1, :, 128:384] - mul3(f_rows, high, low)
    a_ref[...] = jnp.where(lanes >= 64, two, 0.0)
    high, low = split2(mul3(v_one, high, low))
    w_pair[:, 256:512] = high
    w_pair[:, 768:] = low

    def first_of(start, count):
        rows = pl.ds(start, count)
        high, low = split2(rbuf[rows, 0:256])
        wide = mul(high, w_pair[...])
        both = (wide[:, 0:512] + wide[:, 512:]) + mul(low, w_pair[:, 0:512])
        first = both[:, 0:256]
        rest = rbuf[rows, 128:384] - both[:, 256:512]
        rbuf[rows, 0:128] = first[:, 0:128]
        spot = lax.broadcasted_iota(jnp.int32, (count, 128), 1)
        rbuf[rows, 128:256] = jnp.where(spot < 64, first[:, 128:256], rest[:, 0:128])
        rbuf[rows, 256:384] = rest[:, 128:256]
        squares[rows, :] = squares[rows, :] + (first[:, 0:128] * first[:, 0:128] + first[:, 128:256] * first[:, 128:256])

    def round_two(r, _):
        factor_update(a_ref, left_ref, right_ref, r - 1, 64)
        first_of(pl.multiple_of(r * TILE, TILE), TILE)
        factor_round(a_ref, left_ref, right_ref, r, 64)
        return 0

    left_ref[...] = nothing
    right_ref[...] = nothing
    lax.fori_loop(0, ROUNDS, round_two, 0)
    first_of(*CHUNKS[-1])

    v_two = jnp.concatenate([pad, lower_only(a_ref[...], 64)], axis=0).T
    high, low = split2(v_two)
    v_high[...] = high
    v_low[...] = low

    def send(start, count, n):
        rows = pl.ds(start, count)
        return pltpu.make_async_copy(rbuf.at[rows], out_hbm.at[rows], out_sem.at[n])

    def second_of(start, count, n, at):
        rows = pl.ds(start, count)
        second = mul3(rbuf[rows, 128:384], v_high[...], v_low[...])
        spot = lax.broadcasted_iota(jnp.int32, (count, 128), 1)
        rbuf[rows, 128:256] = jnp.where(spot < 64, rbuf[rows, 128:256], second[:, 0:128])
        rbuf[rows, 256:384] = second[:, 128:256]
        send(start, count, n).start()
        square = squares[rows, :] + (second[:, 0:128] * second[:, 0:128] + second[:, 128:256] * second[:, 128:256])
        for q in range(count // 128):
            turned = square[q * 128 : (q + 1) * 128, :].T
            sums[pl.ds(at + q, 1), :] = jnp.sum(turned, axis=0, keepdims=True)

    def round_three(r, _):
        second_of(pl.multiple_of(r * BIG, BIG), BIG, r, r * (BIG // 128))
        return 0

    lax.fori_loop(0, ROWS // BIG, round_three, 0)
    second_of(*CHUNKS[-1], len(CHUNKS) - 1, CHUNKS[-1][0] // 128)

    entry = lax.broadcasted_iota(jnp.int32, (38, 128), 0) * 128 + lax.broadcasted_iota(jnp.int32, (38, 128), 1)
    live = jnp.where(entry < alive, 1.0, 0.0)
    left = live * (diag_ref[...] - sums[...])
    top_left = jnp.max(left)
    top_diag = jnp.max(live * diag_ref[...])
    spot = lax.broadcasted_iota(jnp.int32, (1, 128), 1)
    top_ref[...] = jnp.where(spot < 64, top_left, top_diag)
    for n, (start, count) in enumerate(CHUNKS):
        send(start, count, n).wait()


def panels(everybody, pivots, live_blocks, diag, chol_done, new_cols):
    vmem = pl.BlockSpec(memory_space=pltpu.VMEM)
    hbm = pl.BlockSpec(memory_space=pl.ANY)
    return pl.pallas_call(
        panel_kernel,
        out_shape=(jax.ShapeDtypeStruct((ROWS, COLS), F32), jax.ShapeDtypeStruct((1, 128), F32)),
        in_specs=[vmem, vmem, pl.BlockSpec(memory_space=pltpu.SMEM), vmem, vmem, vmem],
        out_specs=(hbm, vmem),
        scratch_shapes=[
            pltpu.VMEM((ROWS, COLS), F32),
            pltpu.VMEM((ROWS, 128), F32),
            pltpu.VMEM((COLS, K), F32),
            pltpu.VMEM((K, 2 * COLS), BF16),
            pltpu.VMEM((2, ORDER, COLS), F32),
            pltpu.VMEM((ORDER, 256), F32),
            pltpu.VMEM((6 * STEP, 256), BF16),
            pltpu.VMEM((6 * STEP, 256), BF16),
            pltpu.VMEM((256, 256), BF16),
            pltpu.VMEM((256, 256), BF16),
            pltpu.VMEM((256, 1024), BF16),
            pltpu.VMEM((38, 128), F32),
            pltpu.SemaphoreType.DMA((len(CHUNKS),)),
        ],
        compiler_params=pltpu.CompilerParams(vmem_limit_bytes=VMEM_LIMIT),
    )(everybody, pivots, live_blocks, diag, chol_done, new_cols)


def top_kernel(in_ref, out_ref, table, own_sem, send_sem, recv_sem):
    grp, blk = lax.axis_index("grp"), lax.axis_index("blk")
    x, y = lax.div(blk, 4), lax.rem(blk, 4)
    peers = (
        [(lax.rem(grp + k, 8), blk) for k in range(1, 8)],
        [(grp, lax.rem(x + k, 4) * 4 + y) for k in range(1, 4)],
        [(grp, x * 4 + lax.rem(y + k, 4)) for k in range(1, 4)],
    )
    barrier = pltpu.get_barrier_semaphore()
    for group in peers:
        for there in group:
            pl.semaphore_signal(barrier, inc=1, device_id=there, device_id_type=MESH)
    mine = table.at[x, y, grp]
    own = pltpu.make_async_copy(in_ref, mine, own_sem)
    own.start()
    pl.semaphore_wait(barrier, 13)
    sent = []
    for phase, (source, target) in enumerate(
        ((in_ref, mine), (table.at[x, y], table.at[x, y]), (table.at[:, y], table.at[:, y]))
    ):
        if phase == 1:
            own.wait()
        flying = []
        for n, there in enumerate(peers[phase]):
            copy = pltpu.make_async_remote_copy(
                src_ref=source, dst_ref=target, send_sem=send_sem.at[phase, n], recv_sem=recv_sem.at[phase, n],
                device_id=there, device_id_type=MESH,
            )
            copy.start()
            flying.append(copy)
        for copy in flying:
            copy.wait_recv()
        sent += flying
    best = jnp.max(table[...].reshape(128, 128), axis=0, keepdims=True)
    spot = lax.broadcasted_iota(jnp.int32, (1, 128), 1)
    low = -3.0e38
    left = jnp.max(jnp.where(spot < 64, best, low), axis=1, keepdims=True)
    diag = jnp.max(jnp.where(spot < 64, low, best), axis=1, keepdims=True)
    out_ref[...] = jnp.broadcast_to(left / diag, (1, 128))
    for copy in sent:
        copy.wait_send()


def top(mine):
    return pl.pallas_call(
        top_kernel,
        out_shape=jax.ShapeDtypeStruct((1, 128), F32),
        in_specs=[pl.BlockSpec(memory_space=pltpu.VMEM)],
        out_specs=pl.BlockSpec(memory_space=pltpu.VMEM),
        scratch_shapes=[
            pltpu.VMEM((4, 4, 8, 1, 128), F32),
            pltpu.SemaphoreType.DMA,
            pltpu.SemaphoreType.DMA((3, 7)),
            pltpu.SemaphoreType.DMA((3, 7)),
        ],
        compiler_params=pltpu.CompilerParams(collective_id=1, has_side_effects=True, vmem_limit_bytes=2 * 1024 * 1024),
    )(mine)


def body(chol_done, new_cols, diag_entries, pivots, live_blocks):
    slots = pick(pivots, chol_done, new_cols)
    everybody = gather(slots).reshape(128 * SLOT_ROWS, 128)
    diag = diag_entries.reshape(ROWS // 128, 128)
    vectors, mine = panels(everybody, pivots, live_blocks, diag, chol_done, new_cols)
    return vectors, top(mine)[0, 0:1]


def solution(mesh):
    placed = (P(("grp", "blk"), None), P(("grp", "blk"), None), P(("grp", "blk")), P(), P())
    return jax.shard_map(
        body, mesh=mesh, in_specs=placed, out_specs=(P(("grp", "blk"), None), P()), check_vma=False
    )
```

```python
import jax
import jax.numpy as jnp
from jax import lax
from jax.experimental import pallas as pl
from jax.experimental.pallas import tpu as pltpu
from jax.sharding import PartitionSpec as P

MESH = pl.DeviceIdType.MESH
F32 = jnp.float32
BF16 = jnp.bfloat16
ROWS = 4864
K = 512
ORDER = 192
COLS = 384
BLOCK_ROWS = 256
SLOTS = 3
SLOT_ROWS = 40
STEP = 16
ROUNDS = ORDER // STEP
BIG = 768
TILE = 384
CHUNKS = [(i * BIG, BIG) for i in range(ROWS // BIG)] + [(ROWS // BIG * BIG, ROWS % BIG)]
VMEM_LIMIT = 24 * 1024 * 1024
COLOURS = ((0, 13, "yxz"), (13, 13, "xzy"), (26, 13, "zyx"))


def slot_base(panel, slot):
    return slot * 6 if panel == 0 else 18 + slot * 7


def pick_kernel(piv_ref, chol_hbm, cols_hbm, out_ref, cbuf, nbuf, sem):
    me = lax.axis_index("grp") * 16 + lax.axis_index("blk")
    base = me * ROWS
    local = piv_ref[...] - base
    mine = (local >= 0) & (local < ROWS)
    spot = lax.broadcasted_iota(jnp.int32, (2, ORDER), 1)
    key = jnp.where(mine, (spot * 8192 + local).astype(F32), 4.0e6)
    found = []
    for slot in range(SLOTS):
        least = jnp.min(key, axis=1, keepdims=True)
        found.append(least)
        key = jnp.where(key <= least, 4.0e6, key)
    copies = []
    where_row = []
    for panel in range(2):
        for slot in range(SLOTS):
            value = found[slot][panel, 0].astype(jnp.int32)
            row = jnp.where(value < 4000000, value & 8191, 0)
            row = jnp.minimum(row, ROWS - 1)
            group = pl.multiple_of((row // 8) * 8, 8)
            n = panel * SLOTS + slot
            one = pltpu.make_async_copy(chol_hbm.at[pl.ds(group, 8)], cbuf.at[n], sem.at[0, n])
            two = pltpu.make_async_copy(cols_hbm.at[pl.ds(group, 8)], nbuf.at[n], sem.at[1, n])
            one.start()
            two.start()
            copies.append((one, two))
            where_row.append(row - group)
    for panel in range(2):
        for slot in range(SLOTS):
            n = panel * SLOTS + slot
            for copy in copies[n]:
                copy.wait()
            at = slot_base(panel, slot)
            sub = lax.broadcasted_iota(jnp.int32, (8, 128), 0) == where_row[n]
            for c in range(6 if panel == 0 else 7):
                tile = cbuf[n, :, c * 128 : c * 128 + 128] if c < 4 else nbuf[n, :, (c - 4) * 128 : (c - 3) * 128]
                out_ref[at + c : at + c + 1, :] = jnp.sum(jnp.where(sub, tile, 0.0), axis=0, keepdims=True)
    out_ref[39:40, :] = jnp.zeros((1, 128), F32)


def pick(pivots, chol_done, new_cols):
    return pl.pallas_call(
        pick_kernel,
        out_shape=jax.ShapeDtypeStruct((SLOT_ROWS, 128), F32),
        in_specs=[
            pl.BlockSpec(memory_space=pltpu.VMEM),
            pl.BlockSpec(memory_space=pltpu.HBM),
            pl.BlockSpec(memory_space=pltpu.HBM),
        ],
        out_specs=pl.BlockSpec(memory_space=pltpu.VMEM),
        scratch_shapes=[
            pltpu.VMEM((6, 8, K), F32),
            pltpu.VMEM((6, 8, COLS), F32),
            pltpu.SemaphoreType.DMA((2, 6)),
        ],
        compiler_params=pltpu.CompilerParams(vmem_limit_bytes=50 * 1024 * 1024),
    )(pivots, chol_done, new_cols)


def gather_kernel(in_ref, g_ref, own_sem, send_sem, recv_sem, pass_send, pass_recv):
    grp, blk = lax.axis_index("grp"), lax.axis_index("blk")
    at = {"z": lax.div(grp, 2), "x": lax.div(blk, 4), "y": lax.rem(blk, 4)}
    core = lax.rem(grp, 2)

    def device(z, c, x, y):
        return (z * 2 + c, x * 4 + y)

    def beside(axis, k):
        there = dict(at)
        there[axis] = lax.rem(at[axis] + k, 4)
        return device(there["z"], core, there["x"], there["y"])

    partner = device(at["z"], 1 - core, at["x"], at["y"])
    barrier = pltpu.get_barrier_semaphore()
    for axis in "xyz":
        for k in (1, 2, 3):
            pl.semaphore_signal(barrier, inc=1, device_id=beside(axis, k), device_id_type=MESH)
    pl.semaphore_signal(barrier, inc=1, device_id=partner, device_id_type=MESH)
    own = pltpu.make_async_copy(in_ref, g_ref.at[at["z"], core, at["x"], at["y"]], own_sem)
    own.start()
    pl.semaphore_wait(barrier, 10)

    def region(colour, have, fixed):
        first, count, _ = COLOURS[colour]
        pick_at = [slice(None) if a in have else fixed[a] for a in "zxy"]
        return g_ref.at[pick_at[0], core, pick_at[1], pick_at[2], pl.ds(first, count), :]

    flights = {}

    def launch(colour, phase):
        first, count, order = COLOURS[colour]
        have = order[:phase]
        here = region(colour, have, at)
        for k in (3, 2, 1):
            source = in_ref.at[pl.ds(first, count), :] if phase == 0 else here
            copy = pltpu.make_async_remote_copy(
                src_ref=source,
                dst_ref=here,
                send_sem=send_sem.at[colour, phase, k - 1],
                recv_sem=recv_sem.at[colour, phase, k - 1],
                device_id=beside(order[phase], k),
                device_id_type=MESH,
            )
            copy.start()
            flights[colour, phase, k] = copy

    passes = []

    def hand_over(colour, piece, ref):
        copy = pltpu.make_async_remote_copy(
            src_ref=ref,
            dst_ref=ref,
            send_sem=pass_send.at[colour, piece],
            recv_sem=pass_recv.at[colour, piece],
            device_id=partner,
            device_id_type=MESH,
        )
        copy.start()
        passes.append(copy)

    colours = range(len(COLOURS))
    for colour in colours:
        launch(colour, 0)
    own.wait()
    for phase in (1, 2):
        for colour in colours:
            for k in (3, 2, 1):
                flights[colour, phase - 1, k].wait_recv()
            launch(colour, phase)
            if phase == 2:
                hand_over(colour, 0, region(colour, COLOURS[colour][2][:2], at))
    for k in (3, 2, 1):
        for colour in colours:
            flights[colour, 2, k].wait_recv()
            last = COLOURS[colour][2][2]
            there = dict(at)
            there[last] = lax.rem(at[last] + (4 - k), 4)
            hand_over(colour, k, region(colour, COLOURS[colour][2][:2], there))
    for copy in passes:
        copy.wait_recv()
    for copy in passes:
        copy.wait_send()
    for copy in flights.values():
        copy.wait_send()


def gather(slots):
    return pl.pallas_call(
        gather_kernel,
        out_shape=jax.ShapeDtypeStruct((4, 2, 4, 4, SLOT_ROWS, 128), F32),
        in_specs=[pl.BlockSpec(memory_space=pltpu.VMEM)],
        out_specs=pl.BlockSpec(memory_space=pltpu.VMEM),
        scratch_shapes=[
            pltpu.SemaphoreType.DMA,
            pltpu.SemaphoreType.DMA((3, 3, 3)),
            pltpu.SemaphoreType.DMA((3, 3, 3)),
            pltpu.SemaphoreType.DMA((3, 4)),
            pltpu.SemaphoreType.DMA((3, 4)),
        ],
        compiler_params=pltpu.CompilerParams(collective_id=0, has_side_effects=True, vmem_limit_bytes=4 * 1024 * 1024),
        cost_estimate=pl.CostEstimate(flops=20_000_000_000, bytes_accessed=2_700_000, transcendentals=0),
    )(slots)


def split2(a):
    high = a.astype(BF16)
    return high, (a - high.astype(F32)).astype(BF16)


def split3(a):
    high = a.astype(BF16)
    rest = a - high.astype(F32)
    mid = rest.astype(BF16)
    return high, mid, (rest - mid.astype(F32)).astype(BF16)


def mul(a, b):
    return jnp.dot(a, b, preferred_element_type=F32)


def mul3(a, b_high, b_low):
    high, low = split2(a)
    return mul(high, b_high) + (mul(high, b_low) + mul(low, b_high))


def over_lanes(x, lane):
    return jnp.take_along_axis(x, jnp.full((8, 128), lane, jnp.int32), axis=1)


def over_rows(x, row):
    return jnp.broadcast_to(x[row : row + 1, :], (8, 128))


def factor_round(a_ref, left_ref, right_ref, r, off):
    rs = pl.multiple_of(r * STEP, STEP)
    c0 = off + r * STEP
    t = c0 // 128
    l0 = c0 - t * 128
    tl = pl.multiple_of(t * 128, 128)
    lane = lax.broadcasted_iota(jnp.int32, (8, 128), 1)
    sub = lax.broadcasted_iota(jnp.int32, (8, 128), 0)
    raw = [a_ref[pl.ds(rs + 8 * q, 8), pl.ds(tl, 128)] for q in range(2)]
    col = {}
    for j in range(STEP):
        for q in range(j // 8, 2):
            col[j, q] = over_lanes(raw[q], l0 + j)
    row = {}
    for q in range(2):
        for h in range(2):
            x = a_ref[pl.ds(rs + 8 * q, 8), h * 128 : (h + 1) * 128]
            rel = lane + (h * 128) - c0
            unit = jnp.where(rel == sub + 8 * q, 1.0, 0.0)
            row[q, h] = jnp.where((rel >= 0) & (rel < STEP), unit, x)
    for j in range(STEP):
        jq, js = j // 8, j % 8
        scale = lax.rsqrt(over_rows(col[j, jq], js))
        low = {q: col[j, q] * scale for q in range(jq, 2)}
        for m in range(j + 1, STEP):
            times = over_rows(low[m // 8], m % 8)
            for q in range(m // 8, 2):
                col[m, q] = col[m, q] - low[q] * times
        low[jq] = jnp.where(sub > js, low[jq], 0.0)
        for h in range(2):
            lead = over_rows(row[jq, h], js) * scale
            for q in range(jq, 2):
                row[q, h] = row[q, h] - low[q] * lead
            row[jq, h] = jnp.where(sub == js, lead, row[jq, h])
    for q in range(2):
        for h in range(2):
            a_ref[pl.ds(rs + 8 * q, 8), h * 128 : (h + 1) * 128] = row[q, h]
    u = jnp.concatenate([jnp.concatenate([row[q, h] for h in range(2)], axis=1) for q in range(2)], axis=0)
    lanes = lax.broadcasted_iota(jnp.int32, (STEP, 256), 1)
    high, mid, low3 = split3(u)
    h_l, m_l, l_l = split3(jnp.where(lanes >= c0 + STEP, u, 0.0))
    left_ref[...] = jnp.concatenate([h_l, h_l, m_l, m_l, h_l, l_l], axis=0)
    right_ref[...] = jnp.concatenate([high, mid, high, mid, low3, high], axis=0)


def factor_update(a_ref, left_ref, right_ref, r, off):
    c0 = off + r * STEP
    z = lax.dot_general(left_ref[...], right_ref[...], (((0,), (0,)), ((), ())), preferred_element_type=F32)
    rows_i = lax.broadcasted_iota(jnp.int32, (ORDER, 256), 0)
    cols_i = lax.broadcasted_iota(jnp.int32, (ORDER, 256), 1)
    old = (rows_i >= (r + 1) * STEP) & (cols_i >= c0) & (cols_i < c0 + STEP)
    a_ref[...] = jnp.where(old, 0.0, a_ref[...]) - z[off : off + ORDER, :]


def lower_only(a, off):
    row = lax.broadcasted_iota(jnp.int32, (ORDER, 256), 0)
    col = lax.broadcasted_iota(jnp.int32, (ORDER, 256), 1) - off
    return jnp.where((col >= 0) & (col <= row), a, 0.0)


def panel_kernel(g_ref, piv_ref, live_ref, diag_ref, chol, cols, out_hbm, top_ref,
                 rbuf, squares, hmat, ht_pair, head, a_ref, left_ref, right_ref,
                 v_high, v_low, w_pair, sums, out_sem):
    me = lax.axis_index("grp") * 16 + lax.axis_index("blk")
    alive = live_ref[me] * BLOCK_ROWS

    q_i = lax.broadcasted_iota(jnp.int32, (ORDER, ORDER), 1)
    p_i = lax.broadcasted_iota(jnp.int32, (ORDER, ORDER), 0)
    for panel in range(2):
        owner_row = (piv_ref[panel : panel + 1, :] // ROWS).astype(F32)
        owner_all = jnp.broadcast_to(owner_row, (ORDER, ORDER))
        owner = jnp.sum(jnp.where(q_i == p_i, owner_all, 0.0), axis=1, keepdims=True)
        before = (owner_all == owner) & (q_i < p_i)
        rank = jnp.sum(jnp.where(before, 1.0, 0.0), axis=1, keepdims=True)
        dev = lax.broadcasted_iota(jnp.int32, (ORDER, 128), 1).astype(F32)
        hot = jnp.concatenate(
            [jnp.where((dev == owner) & (rank == float(s)), 1.0, 0.0) for s in range(SLOTS)], axis=1
        ).astype(BF16)
        def chunk(c):
            pieces = [g_ref[pl.ds(slot_base(panel, s) + c, 128, stride=SLOT_ROWS), :] for s in range(SLOTS)]
            return jnp.concatenate(pieces, axis=0)

        mine = pl.ds(panel * ORDER, ORDER)
        for c in (0, 2):
            high, low = split2(jnp.concatenate([chunk(c), chunk(c + 1)], axis=1))
            hmat[mine, c * 128 : (c + 2) * 128] = mul(hot, high) + mul(hot, low)
        high, mid, low = split3(jnp.concatenate([chunk(4), chunk(5)], axis=1))
        head[panel, :, 0:256] = mul(hot, high) + (mul(hot, mid) + mul(hot, low))
        if panel == 1:
            high, mid, low = split3(chunk(6))
            head[panel, :, 256:384] = mul(hot, high) + (mul(hot, mid) + mul(hot, low))
    high, low = split2(hmat[...].T)
    ht_pair[:, 0:COLS] = high
    ht_pair[:, COLS:] = low

    lanes = lax.broadcasted_iota(jnp.int32, (ORDER, 256), 1)
    known = mul3(hmat[...], ht_pair[:, 0:COLS], ht_pair[:, COLS:])
    a_ref[...] = jnp.where(lanes < ORDER, head[0, :, 0:256] - known[0:ORDER, 0:256], 0.0)
    head[1, :, :] = head[1, :, :] - known[ORDER:, :]

    def residual_high(start, count):
        rows = pl.ds(start, count)
        both = mul(chol[rows, :].astype(BF16), ht_pair[...])
        rbuf[rows, :] = cols[rows, :] - (both[:, 0:COLS] + both[:, COLS:])

    def residual_low(start, count):
        rows = pl.ds(start, count)
        tile = chol[rows, :]
        left = rbuf[rows, :] - mul(split2(tile)[1], ht_pair[:, 0:COLS])
        spot = lax.broadcasted_iota(jnp.int32, (count, COLS), 0) + start
        rbuf[rows, :] = jnp.where(spot < alive, left, 0.0)
        square = tile * tile
        squares[rows, :] = (square[:, 0:128] + square[:, 128:256]) + (square[:, 256:384] + square[:, 384:512])

    def round_one(r, _):
        start = pl.multiple_of(r * BIG, BIG)
        factor_update(a_ref, left_ref, right_ref, 2 * r - 1, 0)
        residual_high(start, BIG)
        factor_round(a_ref, left_ref, right_ref, 2 * r, 0)
        factor_update(a_ref, left_ref, right_ref, 2 * r, 0)
        residual_low(start, BIG)
        factor_round(a_ref, left_ref, right_ref, 2 * r + 1, 0)
        return 0

    nothing = jnp.zeros((6 * STEP, 256), BF16)
    left_ref[...] = nothing
    right_ref[...] = nothing
    lax.fori_loop(0, ROUNDS // 2, round_one, 0)
    residual_high(*CHUNKS[-1])
    residual_low(*CHUNKS[-1])

    pad = jnp.zeros((64, 256), F32)
    v_one = jnp.concatenate([lower_only(a_ref[...], 0), pad], axis=0).T
    high, low = split2(v_one)
    w_pair[:, 0:256] = high
    w_pair[:, 512:768] = low
    f_rows = mul3(head[1, :, 0:256], high, low)
    f_tr = jnp.concatenate([pad, f_rows], axis=0).T
    high, low = split2(f_tr)
    two = head[1, :, 128:384] - mul3(f_rows, high, low)
    a_ref[...] = jnp.where(lanes >= 64, two, 0.0)
    high, low = split2(mul3(v_one, high, low))
    w_pair[:, 256:512] = high
    w_pair[:, 768:] = low

    def first_of(start, count):
        rows = pl.ds(start, count)
        high, low = split2(rbuf[rows, 0:256])
        wide = mul(high, w_pair[...])
        both = (wide[:, 0:512] + wide[:, 512:]) + mul(low, w_pair[:, 0:512])
        first = both[:, 0:256]
        rest = rbuf[rows, 128:384] - both[:, 256:512]
        rbuf[rows, 0:128] = first[:, 0:128]
        spot = lax.broadcasted_iota(jnp.int32, (count, 128), 1)
        rbuf[rows, 128:256] = jnp.where(spot < 64, first[:, 128:256], rest[:, 0:128])
        rbuf[rows, 256:384] = rest[:, 128:256]
        squares[rows, :] = squares[rows, :] + (first[:, 0:128] * first[:, 0:128] + first[:, 128:256] * first[:, 128:256])

    def round_two(r, _):
        factor_update(a_ref, left_ref, right_ref, r - 1, 64)
        first_of(pl.multiple_of(r * TILE, TILE), TILE)
        factor_round(a_ref, left_ref, right_ref, r, 64)
        return 0

    left_ref[...] = nothing
    right_ref[...] = nothing
    lax.fori_loop(0, ROUNDS, round_two, 0)
    first_of(*CHUNKS[-1])

    v_two = jnp.concatenate([pad, lower_only(a_ref[...], 64)], axis=0).T
    high, low = split2(v_two)
    v_high[...] = high
    v_low[...] = low

    def send(start, count, n):
        rows = pl.ds(start, count)
        return pltpu.make_async_copy(rbuf.at[rows], out_hbm.at[rows], out_sem.at[n])

    def second_of(start, count, n, at):
        rows = pl.ds(start, count)
        second = mul3(rbuf[rows, 128:384], v_high[...], v_low[...])
        spot = lax.broadcasted_iota(jnp.int32, (count, 128), 1)
        rbuf[rows, 128:256] = jnp.where(spot < 64, rbuf[rows, 128:256], second[:, 0:128])
        rbuf[rows, 256:384] = second[:, 128:256]
        send(start, count, n).start()
        square = squares[rows, :] + (second[:, 0:128] * second[:, 0:128] + second[:, 128:256] * second[:, 128:256])
        for q in range(count // 128):
            turned = square[q * 128 : (q + 1) * 128, :].T
            sums[pl.ds(at + q, 1), :] = jnp.sum(turned, axis=0, keepdims=True)

    def round_three(r, _):
        second_of(pl.multiple_of(r * BIG, BIG), BIG, r, r * (BIG // 128))
        return 0

    lax.fori_loop(0, ROWS // BIG, round_three, 0)
    second_of(*CHUNKS[-1], len(CHUNKS) - 1, CHUNKS[-1][0] // 128)

    entry = lax.broadcasted_iota(jnp.int32, (38, 128), 0) * 128 + lax.broadcasted_iota(jnp.int32, (38, 128), 1)
    live = jnp.where(entry < alive, 1.0, 0.0)
    left = live * (diag_ref[...] - sums[...])
    top_left = jnp.max(left)
    top_diag = jnp.max(live * diag_ref[...])
    spot = lax.broadcasted_iota(jnp.int32, (1, 128), 1)
    top_ref[...] = jnp.where(spot < 64, top_left, top_diag)
    for n, (start, count) in enumerate(CHUNKS):
        send(start, count, n).wait()


def panels(everybody, pivots, live_blocks, diag, chol_done, new_cols):
    vmem = pl.BlockSpec(memory_space=pltpu.VMEM)
    hbm = pl.BlockSpec(memory_space=pl.ANY)
    return pl.pallas_call(
        panel_kernel,
        out_shape=(jax.ShapeDtypeStruct((ROWS, COLS), F32), jax.ShapeDtypeStruct((1, 128), F32)),
        in_specs=[vmem, vmem, pl.BlockSpec(memory_space=pltpu.SMEM), vmem, vmem, vmem],
        out_specs=(hbm, vmem),
        scratch_shapes=[
            pltpu.VMEM((ROWS, COLS), F32),
            pltpu.VMEM((ROWS, 128), F32),
            pltpu.VMEM((COLS, K), F32),
            pltpu.VMEM((K, 2 * COLS), BF16),
            pltpu.VMEM((2, ORDER, COLS), F32),
            pltpu.VMEM((ORDER, 256), F32),
            pltpu.VMEM((6 * STEP, 256), BF16),
            pltpu.VMEM((6 * STEP, 256), BF16),
            pltpu.VMEM((256, 256), BF16),
            pltpu.VMEM((256, 256), BF16),
            pltpu.VMEM((256, 1024), BF16),
            pltpu.VMEM((38, 128), F32),
            pltpu.SemaphoreType.DMA((len(CHUNKS),)),
        ],
        compiler_params=pltpu.CompilerParams(vmem_limit_bytes=VMEM_LIMIT),
    )(everybody, pivots, live_blocks, diag, chol_done, new_cols)


def top_kernel(in_ref, out_ref, table, own_sem, send_sem, recv_sem):
    grp, blk = lax.axis_index("grp"), lax.axis_index("blk")
    x, y = lax.div(blk, 4), lax.rem(blk, 4)
    peers = (
        [(lax.rem(grp + k, 8), blk) for k in range(1, 8)],
        [(grp, lax.rem(x + k, 4) * 4 + y) for k in range(1, 4)],
        [(grp, x * 4 + lax.rem(y + k, 4)) for k in range(1, 4)],
    )
    barrier = pltpu.get_barrier_semaphore()
    for group in peers:
        for there in group:
            pl.semaphore_signal(barrier, inc=1, device_id=there, device_id_type=MESH)
    mine = table.at[x, y, grp]
    own = pltpu.make_async_copy(in_ref, mine, own_sem)
    own.start()
    pl.semaphore_wait(barrier, 13)
    sent = []
    for phase, (source, target) in enumerate(
        ((in_ref, mine), (table.at[x, y], table.at[x, y]), (table.at[:, y], table.at[:, y]))
    ):
        if phase == 1:
            own.wait()
        flying = []
        for n, there in enumerate(peers[phase]):
            copy = pltpu.make_async_remote_copy(
                src_ref=source, dst_ref=target, send_sem=send_sem.at[phase, n], recv_sem=recv_sem.at[phase, n],
                device_id=there, device_id_type=MESH,
            )
            copy.start()
            flying.append(copy)
        for copy in flying:
            copy.wait_recv()
        sent += flying
    best = jnp.max(table[...].reshape(128, 128), axis=0, keepdims=True)
    spot = lax.broadcasted_iota(jnp.int32, (1, 128), 1)
    low = -3.0e38
    left = jnp.max(jnp.where(spot < 64, best, low), axis=1, keepdims=True)
    diag = jnp.max(jnp.where(spot < 64, low, best), axis=1, keepdims=True)
    out_ref[...] = jnp.broadcast_to(left / diag, (1, 128))
    for copy in sent:
        copy.wait_send()


def top(mine):
    return pl.pallas_call(
        top_kernel,
        out_shape=jax.ShapeDtypeStruct((1, 128), F32),
        in_specs=[pl.BlockSpec(memory_space=pltpu.VMEM)],
        out_specs=pl.BlockSpec(memory_space=pltpu.VMEM),
        scratch_shapes=[
            pltpu.VMEM((4, 4, 8, 1, 128), F32),
            pltpu.SemaphoreType.DMA,
            pltpu.SemaphoreType.DMA((3, 7)),
            pltpu.SemaphoreType.DMA((3, 7)),
        ],
        compiler_params=pltpu.CompilerParams(collective_id=1, has_side_effects=True, vmem_limit_bytes=2 * 1024 * 1024),
    )(mine)


def body(chol_done, new_cols, diag_entries, pivots, live_blocks):
    slots = pick(pivots, chol_done, new_cols)
    everybody = gather(slots).reshape(128 * SLOT_ROWS, 128)
    diag = diag_entries.reshape(ROWS // 128, 128)
    vectors, mine = panels(everybody, pivots, live_blocks, diag, chol_done, new_cols)
    return vectors, top(mine)[0, 0:1]


def solution(mesh):
    placed = (P(("grp", "blk"), None), P(("grp", "blk"), None), P(("grp", "blk")), P(), P())
    return jax.shard_map(
        body, mesh=mesh, in_specs=placed, out_specs=(P(("grp", "blk"), None), P()), check_vma=False
    )
```
